512 devices in a mesh: blk: 16 (over z_lo, x), leaf: 32 (over y, z_hi, core).
Axes of the slice: x: 4, y: 8, z: 8 (z_hi: 2, z_lo: 4; z = z_hi * 4 + z_lo), core: 2. Of those that a mesh axis runs over, the one named last changes fastest.
Arguments:
- points: bfloat16 [3, 262144], P(None, ('blk', 'leaf')), may hold values from 0 to 1
- test_matrix: bfloat16 [262144, 512], P(('blk', 'leaf')), may hold values from -6 to 6
- near_lists: int32 [1024, 5], P(('blk', 'leaf')), may hold values from 0 to 5, as said below
- leaf_pivots: int32 [512, 256], P(('blk', 'leaf')), may hold values from 0 to 511, as said below
- leaf_proj: bfloat16 [262144, 256], P(('blk', 'leaf')), may hold values from -0.25 to 0.25
- merge_pivots: int32 [3, 512, 256], P(None, ('blk', 'leaf')), may hold values from 0 to 511, as said below
- merge_proj: bfloat16 [3, 512, 512, 256], P(None, ('blk', 'leaf')), as said below
Outputs:
- sample: bfloat16 [262144, 512], P(('blk', 'leaf'))
- top_samples: float32 [131072, 512], P(('blk', 'leaf'))
- top_omega: float32 [131072, 512], P(('blk', 'leaf'))
The draws below stay inside these ranges and needn't reach their ends.
Inputs may be any that keep to these rules, and one draw needn't show every extreme that they name: `near_lists`: the 5 entries of one row are distinct. `leaf_pivots`: the 256 entries of one row are distinct. `merge_pivots`: the 256 entries of one row are distinct; rows [t, n] are equal for all n with the same n // 2^(t+1). `merge_proj`: matrices [t, n] are equal for all n with the same n // 2^(t+1); entries lie within -4 / sqrt(512) to 4 / sqrt(512).
All inputs are finite; a program needn't handle non-finite values.
Results may differ from the reference program's by a relative error of at most 0.0048.
Values may be sent and summed in bfloat16 or wider, within the bound.
A program may use at most 64 MiB of HBM per device.

```python
import math
import jax
import jax.numpy as jnp
from jax import lax

BS = 256
RBD = 2
R = 512
K = 256
NNB = 5
LEVELS = 3
NODES = 512
NBLOCKS = 1024
NPTS = 262144
N_BLK = 16
N_LEAF = 32


def draw_near_lists(key, part):
    key_list = jax.random.split(key, NBLOCKS)
    chosen = jax.vmap(lambda sub_key: jax.random.permutation(sub_key, 3 * RBD))(key_list)
    return chosen[:, :NNB].astype(jnp.int32)


def draw_leaf_pivots(key, part):
    key_list = jax.random.split(key, NODES)
    chosen = jax.vmap(lambda sub_key: jax.random.permutation(sub_key, RBD * BS))(key_list)
    return chosen[:, :K].astype(jnp.int32)


def node_keys(key, tree_level, salt_value):
    base_key = jax.random.fold_in(key, salt_value + tree_level)
    groups = jnp.arange(NODES, dtype=jnp.int32) // 2 ** (tree_level + 1)
    return jax.vmap(lambda group_id: jax.random.fold_in(base_key, group_id))(groups)


def draw_merge_pivots(key, part):
    stacked_levels = []
    for tree_level in range(LEVELS):
        key_list = node_keys(key, tree_level, 11)
        chosen = jax.vmap(lambda sub_key: jax.random.permutation(sub_key, 2 * K))(key_list)
        stacked_levels.append(chosen[:, :K])
    return jnp.stack(stacked_levels).astype(jnp.int32)


def draw_merge_proj(key, part):
    spread_factor = (2.0 * K) ** (-0.5)
    stacked_levels = []
    for tree_level in range(LEVELS):
        key_list = node_keys(key, tree_level, 71)
        values_drawn = jax.vmap(lambda sub_key: jnp.clip(jax.random.normal(sub_key, (2 * K, K), jnp.float32), -3.9, 3.9))(key_list)
        stacked_levels.append(values_drawn * spread_factor)
    return jnp.stack(stacked_levels).astype(jnp.bfloat16)


def block_levels(stream_key, shape, shards, low, high):
    def one(axis_at, blocks):
        draws = jax.random.uniform(jax.random.fold_in(jax.random.fold_in(stream_key, 6), axis_at), (blocks,), jnp.float32, low / len(shards), high / len(shards))
        return jnp.repeat(jnp.exp(draws), shape[axis_at] // blocks).reshape((-1,) + (1,) * (len(shape) - axis_at - 1))

    gain = one(*shards[0])
    for cut in shards[1:]:
        gain = gain * one(*cut)
    return gain


def normal_values(own_key, extent, scale, limit, pieces=(), kind=jnp.bfloat16):
    result = jax.random.normal(own_key, extent, jnp.float32) * scale
    if len(pieces) > 0:
        result = block_levels(own_key, extent, pieces, -0.22, 0.18) * result
    return jnp.clip(result, min=-limit, max=limit).astype(kind)


def setup_inputs(seed: int = 0) -> dict:
    seeds = jax.random.split(jax.random.key(seed), 8)
    return {
        "points": jnp.clip(1.0 * jax.random.uniform(seeds[0], (3, NPTS), jnp.float32) ** block_levels(seeds[0], (3, NPTS), ((1, 512),), -0.2, 0.2), 0.0, 1.0).astype(jnp.bfloat16),
        "test_matrix": normal_values(seeds[1], (NPTS, R), 1.0, 6.0, ((0, 512),)),
        "near_lists": draw_near_lists(jax.random.fold_in(seeds[7], 71), 0),
        "leaf_pivots": draw_leaf_pivots(jax.random.fold_in(seeds[7], 71), 0),
        "leaf_proj": normal_values(seeds[4], (NPTS, K), (RBD * BS) ** -0.5, 0.25, ((0, 512),)),
        "merge_pivots": draw_merge_pivots(jax.random.fold_in(seeds[7], 71), 0),
        "merge_proj": draw_merge_proj(jax.random.fold_in(seeds[7], 71), 0),
    }


SPREAD = 25.0

def kernel_block(row_points, col_points):
    offsets = row_points[..., :, :, None] - col_points[..., :, None, :]
    return jnp.exp(-SPREAD * lax.optimization_barrier(jnp.sum(offsets * offsets, axis=-3)))

def select_rows(matrix_in, index_in):
    return matrix_in[index_in]

def select_columns(matrix_in, index_in):
    return matrix_in[:, index_in]

def reference(points, test_matrix, near_lists, leaf_pivots, leaf_proj, merge_pivots, merge_proj):
    near_amp = 9.0 / math.sqrt(NNB * BS)
    far_amp = 3.0 / math.sqrt(K)
    row_count = RBD * BS
    points_grid = points.astype(jnp.float32).reshape(3, N_BLK, N_LEAF, RBD, BS)
    matrix_grid = test_matrix.reshape(N_BLK, N_LEAF, RBD, BS, R)
    lists_grid = near_lists.reshape(N_BLK, N_LEAF, RBD, NNB)
    pivots_grid = leaf_pivots.reshape(N_BLK, N_LEAF, K)
    proj_grid = leaf_proj.reshape(N_BLK, N_LEAF, row_count, K)

    def one_device(device_index):
        blk_index = device_index // N_LEAF
        leaf_index = device_index % N_LEAF
        sources = [(blk_index + N_BLK - 1) % N_BLK, blk_index, (blk_index + 1) % N_BLK]
        wide_matrix = jnp.concatenate([matrix_grid[source, leaf_index] for source in sources], axis=0)
        wide_points = jnp.concatenate([jnp.transpose(points_grid[:, source, leaf_index], (1, 0, 2)) for source in sources], axis=0)
        own_points = jnp.transpose(points_grid[:, blk_index, leaf_index], (1, 0, 2))
        lists_here = lists_grid[blk_index, leaf_index]
        full_sum = jnp.zeros((RBD, BS, R), jnp.float32)
        remote_sum = jnp.zeros((RBD, BS, R), jnp.float32)
        for entry_slot in range(NNB):
            candidate = lists_here[:, entry_slot]
            near_block = (near_amp * kernel_block(own_points, wide_points[candidate])).astype(jnp.bfloat16)
            term_block = jnp.einsum('ipq,iqr->ipr', near_block.astype(jnp.float32), wide_matrix[candidate].astype(jnp.float32))
            is_remote = (candidate // RBD != 1).astype(jnp.float32)[:, None, None]
            full_sum = full_sum + term_block
            remote_sum = remote_sum + is_remote * term_block
        remote_rows = remote_sum.reshape(row_count, R)
        pivots = pivots_grid[blk_index, leaf_index]
        samples = remote_rows[pivots]
        skeleton = points_grid[:, blk_index, leaf_index].reshape(3, row_count)[:, pivots]
        compressed = jnp.dot(proj_grid[blk_index, leaf_index].T, matrix_grid[blk_index, leaf_index].reshape(row_count, R), preferred_element_type=jnp.float32)
        return (full_sum.reshape(row_count, R).astype(jnp.bfloat16), samples, compressed, skeleton)
    sample, samples, compressed, skeleton = lax.map(one_device, jnp.arange(NODES, dtype=jnp.int32))
    samples = samples.reshape(N_BLK, N_LEAF, K, R)
    compressed = compressed.reshape(N_BLK, N_LEAF, K, R)
    skeleton = skeleton.reshape(N_BLK, N_LEAF, 3, K)
    pivots_all = merge_pivots.reshape(LEVELS, N_BLK, N_LEAF, K)
    proj_all = merge_proj.reshape(LEVELS, N_BLK, N_LEAF, 2 * K, K)
    highest = lax.Precision.HIGHEST
    for tree_level in range(1, LEVELS + 1):
        group_count = N_LEAF >> tree_level
        paired = samples.reshape(N_BLK, group_count, 2, K, R)
        paired_comp = compressed.reshape(N_BLK, group_count, 2, K, R)
        paired_skel = skeleton.reshape(N_BLK, group_count, 2, 3, K)
        coupling = far_amp * kernel_block(paired_skel[:, :, 0], paired_skel[:, :, 1])
        upper_half = paired[:, :, 0] - jnp.einsum('bnpq,bnqr->bnpr', coupling, paired_comp[:, :, 1], precision=highest)
        lower_half = paired[:, :, 1] - jnp.einsum('bnqp,bnqr->bnpr', coupling, paired_comp[:, :, 0], precision=highest)
        stacked = jnp.concatenate([upper_half, lower_half], axis=2)
        pivots = pivots_all[tree_level - 1].reshape(N_BLK, group_count, 2 ** tree_level, K)[:, :, 0]
        projection = proj_all[tree_level - 1].reshape(N_BLK, group_count, 2 ** tree_level, 2 * K, K)[:, :, 0].astype(jnp.float32)
        samples = jax.vmap(jax.vmap(select_rows))(stacked, pivots)
        joined = jnp.concatenate([paired_skel[:, :, 0], paired_skel[:, :, 1]], axis=3)
        skeleton = jax.vmap(jax.vmap(select_columns))(joined, pivots)
        compressed = jnp.einsum('bnqp,bnqr->bnpr', projection, paired_comp.reshape(N_BLK, group_count, 2 * K, R), precision=highest)
    repeats = 2 ** LEVELS
    top_samples = jnp.repeat(samples, repeats, axis=1).reshape(NODES * K, R)
    top_omega = jnp.repeat(compressed, repeats, axis=1).reshape(NODES * K, R)
    return (sample.reshape(NPTS, R), top_samples, top_omega)
```

```python
import functools
import math

import jax
import jax.numpy as jnp
from jax import lax
from jax.experimental import pallas as pl
from jax.experimental.pallas import tpu as pltpu
from jax.sharding import PartitionSpec as P

SPREAD = 25.0
MESH = pl.DeviceIdType.MESH
BF = jnp.bfloat16
F32 = jnp.float32
FAR = -512.0
SCALE = 2.0 * SPREAD / math.log(2.0)
N_CHUNK = 4


def tdot(a, b):
    return lax.dot_general(a, b, (((0,), (0,)), ((), ())), preferred_element_type=F32)


def mdot(a, b):
    return jnp.dot(a, b, preferred_element_type=F32)


def rows_of(shape, entries):
    index = lax.broadcasted_iota(jnp.int32, shape, 0)
    result = jnp.zeros(shape, F32)
    for at, value in entries:
        result = jnp.where(index == at, value, result)
    return result


def features(points, block_rows):
    count = points.shape[1]
    x, y, z = points[0:1], points[1:2], points[2:3]
    half = 0.5 * (x * x + y * y + z * z)
    high = half.astype(BF).astype(F32)
    mid = (half - high).astype(BF).astype(F32)
    low = (half - high - mid).astype(BF).astype(F32)
    lane = lax.broadcasted_iota(jnp.int32, (1, count), 1)
    in_first = (lane < block_rows).astype(F32)
    return rows_of(
        (16, count),
        [(0, x), (1, y), (2, z), (3, 1.0), (4, 1.0), (5, 1.0), (6, high), (7, mid), (8, low),
         (9, in_first), (10, 1.0 - in_first)],
    )


def source_side(feat, penalties):
    r = lax.broadcasted_iota(jnp.int32, (16, 16), 0)
    c = lax.broadcasted_iota(jnp.int32, (16, 16), 1)
    same = (r == c) & (r < 3)
    swap = ((r >= 3) & (r < 6) & (c == r + 3)) | ((r >= 6) & (r < 9) & (c == r - 3))
    form = jnp.where(same, 1.0, jnp.where(swap, -1.0, 0.0)).astype(BF)
    turned = mdot(form, feat)
    return (turned + rows_of(turned.shape, penalties + [(11, FAR)])).astype(BF)


def only_valid(feat):
    index = lax.broadcasted_iota(jnp.int32, feat.shape, 0)
    return jnp.where(index == 11, 1.0 - feat[3:4], feat).astype(BF)


def kernel_of(target, source, amp):
    return jnp.exp2(tdot(target, source) * SCALE + math.log2(amp))


def one_hot(pivots, offset, count):
    k = lax.broadcasted_iota(jnp.int32, (count, pivots.shape[1]), 0)
    return jnp.where(k == pivots - offset, 1.0, 0.0).astype(BF)


def body(n_blk, near_amp, far_amp,
         lists, points, pivots, tree_pivots, test_hbm, proj_hbm, tree_hbm,
         sample, top, omega,
         wide, proj, tree, near, part, feat_own, feat_in, u0, v0, u1, v1, u2, v2,
         c0, c1, c2, e2, e3, f_out, f_core, g_out, g_in, h_out, h_in, own_sum,
         local_sem, send_sem, recv_sem):
    b = lax.axis_index("blk")
    l = lax.axis_index("leaf")
    core = lax.rem(l, 2)
    bits = [lax.rem(l // (1 << t), 2) for t in range(3)]
    peers = {
        "next": {"blk": lax.rem(b + 1, n_blk), "leaf": l},
        "prev": {"blk": lax.rem(b + n_blk - 1, n_blk), "leaf": l},
    }
    for t in range(3):
        peers[t] = {"blk": b, "leaf": l + (1 << t) - (2 << t) * bits[t]}
    barrier = pltpu.get_barrier_semaphore()
    for peer in peers.values():
        pl.semaphore_signal(barrier, inc=1, device_id=peer, device_id_type=MESH)

    rows = proj.shape[0]
    block_rows = rows // 2
    rank = proj.shape[1]
    half_rank = rank // 2
    cols = wide.shape[1] // N_CHUNK
    used = [0]
    pending = []

    def send(src, dst, peer):
        at = used[0]
        used[0] += 1
        copy = pltpu.make_async_remote_copy(
            src_ref=src, dst_ref=dst, send_sem=send_sem.at[at], recv_sem=recv_sem.at[at],
            device_id=peers[peer], device_id_type=MESH)
        copy.start()
        pending.append(copy)
        return copy

    fetch = [
        pltpu.make_async_copy(test_hbm, wide.at[pl.ds(rows, rows), :], local_sem.at[0]),
        pltpu.make_async_copy(proj_hbm, proj, local_sem.at[1]),
        pltpu.make_async_copy(tree_hbm, tree, local_sem.at[2]),
    ]
    for copy in fetch:
        copy.start()

    own = features(points[...].astype(F32), block_rows).astype(BF)
    feat_own[...] = own
    skeleton = mdot(own, one_hot(pivots[...], 0, rows)).astype(BF)
    u0[...] = skeleton
    pick_own = [one_hot(tree_pivots[t], rank * bits[t], rank) for t in range(3)]
    pick_sib = [one_hot(tree_pivots[t], rank * (1 - bits[t]), rank) for t in range(3)]

    pl.semaphore_wait(barrier, len(peers))

    far_feat = [send(feat_own, feat_in.at[0], "next"), send(feat_own, feat_in.at[1], "prev")]
    u0_copy = send(u0, v0, 0)
    stream = []
    for j in range(N_CHUNK):
        at = pl.ds(j * cols, cols)
        stream.append((
            send(test_hbm.at[:, at], wide.at[pl.ds(0, rows), at], "next"),
            send(test_hbm.at[:, at], wide.at[pl.ds(2 * rows, rows), at], "prev"),
        ))

    fetch[0].wait()
    fetch[1].wait()
    c0[...] = tdot(proj[...], wide[rows:2 * rows, :]).astype(BF)
    c0_copy = send(c0, wide.at[pl.ds(3 * rows, rank), :], 0)

    def hit(i, c):
        found = lists[i, 0] == c
        for e in range(1, lists.shape[1]):
            found = found | (lists[i, e] == c)
        return jnp.where(found, 0.0, FAR)

    def near_source(feat, group):
        lane = lax.broadcasted_iota(jnp.int32, (1, rows), 1)
        penalties = [
            (9 + i, jnp.where(lane < block_rows, hit(i, 2 * group), hit(i, 2 * group + 1)))
            for i in range(2)
        ]
        return source_side(feat, penalties)

    near[:, rows:2 * rows] = kernel_of(own, near_source(own, 1), near_amp).astype(BF)
    w1 = mdot(skeleton, pick_own[0])
    w2 = mdot(w1.astype(BF), pick_own[1])
    w3 = mdot(w2.astype(BF), pick_own[2])
    mine = only_valid(w3)

    fetch[2].wait()
    u0_copy.wait_recv()
    sib0 = v0[...]
    level1 = (w1 + mdot(sib0, pick_sib[0])).astype(BF)
    u1[...] = level1
    c0_copy.wait_recv()

    def merged(t, mine_ref, sib_ref):
        left = tree[t, pl.ds(pl.multiple_of(rank * bits[t], rank), rank), :]
        right = tree[t, pl.ds(pl.multiple_of(rank * (1 - bits[t]), rank), rank), :]
        return tdot(left, mine_ref[...]) + tdot(right, sib_ref[...])

    low_half = pl.ds(pl.multiple_of(core * half_rank, half_rank), half_rank)
    own_rows = pl.ds(pl.multiple_of(rank + core * half_rank, half_rank), half_rank)
    c1[rank:, :] = merged(0, c0, wide.at[pl.ds(3 * rows, rank), :]).astype(BF)
    u1_copy = send(u1, v1, 1)
    c1_copy = send(c1.at[own_rows, :], c1.at[low_half, :], 1)

    part[:, 2 * rows:] = -kernel_of(mine, source_side(sib0, []), far_amp).astype(BF)
    for copy in far_feat:
        copy.wait_recv()
    for g in range(2):
        source = near_source(feat_in[g], 2 * g)
        part[:, g * rows:(g + 1) * rows] = kernel_of(mine, source, near_amp).astype(BF)
        near[:, 2 * g * rows:(2 * g + 1) * rows] = kernel_of(own, source, near_amp).astype(BF)

    f_copy, g_copy, h_copy, t_copy = {}, {}, {}, {}
    far_half = pl.ds(pl.multiple_of((1 - core) * half_rank, half_rank), half_rank)

    def leaf_rows(j):
        at = slice(j * cols, (j + 1) * cols)
        for copy in stream[j]:
            copy.wait_recv()
        total = mdot(part[:, :rows], wide[:rows, at]) + mdot(part[:, rows:], wide[2 * rows:, at])
        f_out[j] = total.astype(BF)
        f_copy[j] = send(f_out.at[j, far_half, :], f_core.at[j], 0)

    def block_rows_sum(j):
        at = slice(j * cols, (j + 1) * cols)
        sample[:, at] = mdot(near[...], wide[:3 * rows, at]).astype(BF)

    def chip_rows(j):
        f_copy[j].wait_recv()
        g_out[j] = (f_out[j, low_half, :].astype(F32) + f_core[j].astype(F32)).astype(BF)
        g_copy[j] = send(g_out.at[j], g_in.at[j], 1)

    def node_rows(j):
        at = slice(j * cols, (j + 1) * cols)
        g_copy[j].wait_recv()
        total = g_out[j].astype(F32) + g_in[j].astype(F32) - e2[:, at]
        own_sum[j] = total
        h_out[j] = total.astype(BF)
        h_copy[j] = send(h_out.at[j], h_in.at[j], 2)

    def top_rows(j):
        at = slice(j * cols, (j + 1) * cols)
        h_copy[j].wait_recv()
        top[low_half, at] = own_sum[j] + h_in[j].astype(F32) - e3[:, at]
        place = top.at[low_half, pl.ds(j * cols, cols)]
        t_copy[j] = send(place, place, 0)

    def halves(feat):
        return jnp.where(core == 0, feat[:, :half_rank], feat[:, half_rank:])

    def correction(mine_feat, sib_feat, sib_skel, own_skel, stacked):
        weights = jnp.concatenate(
            [kernel_of(only_valid(halves(mine_feat)), source_side(sib_skel, []), far_amp).astype(BF),
             kernel_of(only_valid(halves(sib_feat)), source_side(own_skel, []), far_amp).astype(BF)],
            axis=1)
        return mdot(weights, stacked[...])

    leaf_rows(0)
    block_rows_sum(0)
    chip_rows(0)
    leaf_rows(1)
    chip_rows(1)
    block_rows_sum(1)

    u1_copy.wait_recv()
    sib1 = v1[...]
    from_own = mdot(level1, pick_own[1])
    from_sib = mdot(sib1, pick_sib[1])
    level2 = (from_own + from_sib).astype(BF)
    u2[...] = level2
    u2_copy = send(u2, v2, 2)
    c1_copy.wait_recv()
    c1_share = send(c1.at[low_half, :], c1.at[low_half, :], 0)
    x2 = mdot(from_own.astype(BF), pick_own[2])
    y2 = mdot(from_sib.astype(BF), pick_own[2])

    leaf_rows(2)
    chip_rows(2)

    c1_share.wait_recv()
    c2[rank:, :] = merged(1, c1.at[pl.ds(rank, rank), :], c1.at[pl.ds(0, rank), :]).astype(BF)
    c2_copy = send(c2.at[own_rows, :], c2.at[low_half, :], 2)
    e2[...] = correction(x2, y2, sib1, level1, c1)
    block_rows_sum(2)
    node_rows(0)
    node_rows(1)

    leaf_rows(3)
    chip_rows(3)
    block_rows_sum(3)

    u2_copy.wait_recv()
    sib2 = v2[...]
    y3 = mdot(sib2, pick_sib[2])
    c2_copy.wait_recv()
    c2_share = send(c2.at[low_half, :], c2.at[low_half, :], 0)
    node_rows(2)
    c2_share.wait_recv()
    e3[...] = correction(x2 + y2, y3, sib2, level2, c2)
    top_rows(0)
    top_rows(1)
    omega[...] = merged(2, c2.at[pl.ds(rank, rank), :], c2.at[pl.ds(0, rank), :])
    node_rows(3)
    top_rows(2)
    top_rows(3)
    for j in range(N_CHUNK):
        t_copy[j].wait_recv()
    for copy in pending:
        copy.wait_send()


def on_device(n_blk, points, test_matrix, near_lists, leaf_pivots, leaf_proj, merge_pivots, merge_proj):
    rows, cols = test_matrix.shape
    rank = leaf_pivots.shape[1]
    slots = near_lists.shape[1]
    near_amp = 9.0 / math.sqrt(slots * (rows // near_lists.shape[0]))
    far_amp = 3.0 / math.sqrt(rank)
    half = rank // 2
    chunk = cols // N_CHUNK
    vmem = pl.BlockSpec(memory_space=pltpu.VMEM)
    anyw = pl.BlockSpec(memory_space=pl.ANY)
    copies = 14 + 6 * N_CHUNK
    scratch = [
        pltpu.VMEM((3 * rows + rank, cols), BF),
        pltpu.VMEM((rows, rank), BF),
        pltpu.VMEM((3, 2 * rank, rank), BF),
        pltpu.VMEM((rows, 3 * rows), BF),
        pltpu.VMEM((rank, 2 * rows + rank), BF),
        pltpu.VMEM((16, rows), BF),
        pltpu.VMEM((2, 16, rows), BF),
    ] + [pltpu.VMEM((16, rank), BF)] * 6 + [
        pltpu.VMEM((rank, cols), BF),
        pltpu.VMEM((2 * rank, cols), BF),
        pltpu.VMEM((2 * rank, cols), BF),
        pltpu.VMEM((half, cols), F32),
        pltpu.VMEM((half, cols), F32),
        pltpu.VMEM((N_CHUNK, rank, chunk), BF),
    ] + [pltpu.VMEM((N_CHUNK, half, chunk), BF)] * 5 + [
        pltpu.VMEM((N_CHUNK, half, chunk), F32),
        pltpu.SemaphoreType.DMA((3,)),
        pltpu.SemaphoreType.DMA((copies,)),
        pltpu.SemaphoreType.DMA((copies,)),
    ]
    return pl.pallas_call(
        functools.partial(body, n_blk, near_amp, far_amp),
        name="hss",
        out_shape=(
            jax.ShapeDtypeStruct((rows, cols), BF),
            jax.ShapeDtypeStruct((rank, cols), F32),
            jax.ShapeDtypeStruct((rank, cols), F32),
        ),
        in_specs=[pl.BlockSpec(memory_space=pltpu.SMEM), vmem, vmem, vmem, anyw, anyw, anyw],
        out_specs=(vmem, vmem, vmem),
        scratch_shapes=scratch,
        compiler_params=pltpu.CompilerParams(
            collective_id=0, has_side_effects=True, vmem_limit_bytes=48 << 20),
    )(near_lists, points, leaf_pivots, merge_pivots, test_matrix, leaf_proj,
      merge_proj.reshape(merge_proj.shape[0], merge_proj.shape[2], merge_proj.shape[3]))


def solution(mesh):
    placed = (
        P(None, ("blk", "leaf")),
        P(("blk", "leaf"), None),
        P(("blk", "leaf"), None),
        P(("blk", "leaf"), None),
        P(("blk", "leaf"), None),
        P(None, ("blk", "leaf"), None),
        P(None, ("blk", "leaf"), None, None),
    )
    return jax.shard_map(
        functools.partial(on_device, mesh.shape["blk"]),
        mesh=mesh,
        in_specs=placed,
        out_specs=(P(("blk", "leaf"), None), P(("blk", "leaf"), None), P(("blk", "leaf"), None)),
        check_vma=False,
    )
```

```python
import functools
import math

import jax
import jax.numpy as jnp
from jax import lax
from jax.experimental import pallas as pl
from jax.experimental.pallas import tpu as pltpu
from jax.sharding import PartitionSpec as P

SPREAD = 25.0
MESH = pl.DeviceIdType.MESH
BF = jnp.bfloat16
F32 = jnp.float32
FAR = -512.0
SCALE = 2.0 * SPREAD / math.log(2.0)


def tdot(a, b):
    return lax.dot_general(a, b, (((0,), (0,)), ((), ())), preferred_element_type=F32)


def mdot(a, b):
    return jnp.dot(a, b, preferred_element_type=F32)


def rows_of(shape, entries):
    index = lax.broadcasted_iota(jnp.int32, shape, 0)
    result = jnp.zeros(shape, F32)
    for at, value in entries:
        result = jnp.where(index == at, value, result)
    return result


PLACES = ((9, 10), (14, 15), (12, 13))


def features(points, lists, block_rows):
    count = points.shape[1]
    x, y, z = points[0:1], points[1:2], points[2:3]
    half = 0.5 * (x * x + y * y + z * z)
    high = half.astype(BF).astype(F32)
    mid = (half - high).astype(BF).astype(F32)
    low = (half - high - mid).astype(BF).astype(F32)
    lane = lax.broadcasted_iota(jnp.int32, (1, count), 1)
    entries = [(0, x), (1, y), (2, z), (3, 1.0), (4, 1.0), (5, 1.0), (6, high), (7, mid), (8, low)]
    for place, at in enumerate(PLACES):
        for j in range(2):
            listed = jnp.max((lists == 2 * place + j).astype(F32), axis=1, keepdims=True)
            skipped = (1.0 - listed) * FAR
            entries.append((at[j], jnp.where(lane < block_rows, skipped[0:1], skipped[1:2])))
    return rows_of((16, count), entries)


def source_side(feat, place=None):
    r = lax.broadcasted_iota(jnp.int32, (16, 16), 0)
    c = lax.broadcasted_iota(jnp.int32, (16, 16), 1)
    same = (r == c) & (r < 3)
    swap = ((r >= 3) & (r < 6) & (c == r + 3)) | ((r >= 6) & (r < 9) & (c == r - 3))
    form = jnp.where(same, 1.0, jnp.where(swap, -1.0, 0.0)).astype(BF)
    turned = mdot(form, feat)
    count = feat.shape[1]
    extra = [(11, FAR)]
    if place is not None:
        lane = lax.broadcasted_iota(jnp.int32, (1, count), 1)
        first = (lane < count // 2).astype(F32)
        extra += [(PLACES[place][0], first), (PLACES[place][1], 1.0 - first)]
    return (turned + rows_of(turned.shape, extra)).astype(BF)


def only_valid(feat):
    index = lax.broadcasted_iota(jnp.int32, feat.shape, 0)
    return jnp.where(index == 11, 1.0 - feat[3:4], feat).astype(BF)


def kernel_of(target, source, amp):
    return jnp.exp2(tdot(target, source) * SCALE + math.log2(amp))


def one_hot(pivots, offset, count):
    k = lax.broadcasted_iota(jnp.int32, (count, pivots.shape[1]), 0)
    return jnp.where(k == pivots - offset, 1.0, 0.0).astype(BF)


def body(n_blk, near_amp, far_amp,
         lists_hbm, points_hbm, pivots_hbm, tree_pivots_hbm, test_hbm, proj_hbm, tree_hbm,
         sample, top, omega,
         lists, points, pivots, tree_pivots, proj, tree, wide, stack, near, far,
         feat_out, feat_in, kept_out, kept_in, chip_out, z_in, y_in, yz_in,
         o_out, o_core, o_sum, o_q, o_part, o_y, o_send, o_z, o_t, o_ty, o_tc,
         r_out, r_core, r_sum, r_x, e_out, e_core,
         g_half, g_own, g_part, g_y, g_out, g_z, g_t, g_ty, g_tc,
         local_sem, send_sem, recv_sem):
    b = lax.axis_index("blk")
    l = lax.axis_index("leaf")
    bits = [lax.rem(l // (1 << t), 2) for t in range(3)]
    step = [(1 << t) - (2 << t) * bits[t] for t in range(3)]
    peers = {
        "next": {"blk": lax.rem(b + 1, n_blk), "leaf": l},
        "prev": {"blk": lax.rem(b + n_blk - 1, n_blk), "leaf": l},
        "core": {"blk": b, "leaf": l + step[0]},
        "z": {"blk": b, "leaf": l + step[1]},
        "y": {"blk": b, "leaf": l + step[2]},
        "yz": {"blk": b, "leaf": l + step[1] + step[2]},
    }
    barrier = pltpu.get_barrier_semaphore()
    for peer in peers.values():
        pl.semaphore_signal(barrier, inc=1, device_id=peer, device_id_type=MESH)

    rows, rank = proj.shape
    block_rows = rows // 2
    half = rank // 2
    quarter = half // 2
    pending = []

    def send(src, dst, peer):
        at = len(pending)
        copy = pltpu.make_async_remote_copy(
            src_ref=src, dst_ref=dst, send_sem=send_sem.at[at], recv_sem=recv_sem.at[at],
            device_id=peers[peer], device_id_type=MESH)
        copy.start()
        pending.append(copy)
        return copy

    def fetch(at, src, dst):
        copy = pltpu.make_async_copy(src, dst, local_sem.at[at])
        copy.start()
        return copy

    small = [fetch(0, lists_hbm, lists), fetch(1, points_hbm, points),
             fetch(2, pivots_hbm, pivots), fetch(3, tree_pivots_hbm, tree_pivots)]
    large = [fetch(4, test_hbm, wide.at[pl.ds(rows, rows), :]), fetch(5, proj_hbm, proj),
             fetch(6, tree_hbm, tree)]

    near_half = pl.ds(pl.multiple_of(bits[0] * half, half), half)
    far_half = pl.ds(pl.multiple_of((1 - bits[0]) * half, half), half)
    near_quarter = pl.ds(pl.multiple_of(bits[2] * quarter, quarter), quarter)
    far_quarter = pl.ds(pl.multiple_of((1 - bits[2]) * quarter, quarter), quarter)

    def quarter_of(core, part):
        return pl.ds(pl.multiple_of(core * half + part * quarter, quarter), quarter)

    top_quarter = quarter_of(bits[0], bits[2])

    for copy in small:
        copy.wait()
    own = features(points[...].astype(F32), lists[...], block_rows).astype(BF)
    skeleton = mdot(own, one_hot(pivots[...], 0, rows)).astype(BF)
    kept = skeleton
    for t in range(3):
        kept = mdot(kept, one_hot(tree_pivots[t], rank * bits[t], rank)).astype(BF)
        kept_out[:, t * rank:(t + 1) * rank] = kept
    feat_out[:, :rows] = own
    feat_out[:, rows:] = only_valid(kept.astype(F32))

    pl.semaphore_wait(barrier, len(peers))

    kept_copy = send(kept_out, kept_in, "core")
    feat_copy = [send(feat_out, feat_in.at[0], "next"), send(feat_out, feat_in.at[1], "prev")]

    def stream_chunk(start, size):
        at = pl.ds(start, size)
        return [
            send(test_hbm.at[:, at], wide.at[pl.ds(0, rows), at], "next"),
            send(test_hbm.at[:, at], wide.at[pl.ds(2 * rows, rows), at], "prev"),
        ]

    cols = wide.shape[1]
    stream = [stream_chunk(0, cols // 4)]

    for copy in large:
        copy.wait()
    share = tdot(proj[...], wide[rows:2 * rows, :])

    kept_copy.wait_recv()
    chip = kept_out[...].astype(F32) + kept_in[...].astype(F32)
    level1 = chip[:, :rank].astype(BF)
    chip_out[...] = chip[:, rank:].astype(BF)
    chip_copy = [
        send(chip_out, z_in, "z"),
        send(chip_out.at[:, pl.ds(rank, rank)], yz_in, "yz"),
        send(chip_out.at[:, pl.ds(rank, rank)], y_in, "y"),
    ]

    for t in range(3):
        high = share.astype(BF)
        low = (share - high.astype(F32)).astype(BF)
        stack[t * rank:(t + 1) * rank, :] = high
        child = tree[t, 0, pl.ds(pl.multiple_of(rank * bits[t], rank), rank), :]
        share = tdot(child, high) + tdot(child, low)
    o_out[...] = share
    o_core_copy = send(o_out.at[far_half, :], o_core, "core")

    for copy in feat_copy:
        copy.wait_recv()
    for side, place in ((0, 2), (1, 0)):
        weights = kernel_of(feat_in[side, :, rows:], source_side(own, place), near_amp).astype(BF)
        r_out[side] = mdot(weights, wide[rows:2 * rows, :]).astype(BF)
    r_core_copy = send(r_out.at[:, far_half, :], r_core, "core")

    o_core_copy.wait_recv()
    o_sum[...] = o_out[near_half, :] + o_core[...]
    o_part[...] = o_sum[far_quarter, :].astype(BF)
    o_y_copy = send(o_part, o_y, "y")

    r_core_copy.wait_recv()
    r_sum[...] = (r_out[:, near_half, :].astype(F32) + r_core[...].astype(F32)).astype(BF)
    r_x_copy = [send(r_sum.at[1], r_x.at[0], "next"), send(r_sum.at[0], r_x.at[1], "prev")]
    stream.append(stream_chunk(cols // 4, cols // 4))
    stream.append(stream_chunk(cols // 2, cols // 2))

    def weigh(t, feat, source):
        at = slice(t * rank, (t + 1) * rank)
        far[:, at] = kernel_of(only_valid(feat), source_side(source), far_amp).astype(BF)

    def near_part(place, feat):
        at = slice(place * rows, (place + 1) * rows)
        near[:, at] = kernel_of(own, source_side(feat, place), near_amp).astype(BF)

    weigh(0, kept_in[:, 2 * rank:].astype(F32), skeleton)
    near_part(1, own)

    o_y_copy.wait_recv()
    o_q[...] = o_sum[near_quarter, :] + o_y[...].astype(F32)
    o_send[...] = o_q[...].astype(BF)
    o_z_copy = send(o_send, o_z, "z")

    chip_copy[0].wait_recv()
    weigh(1, z_in[:, rank:].astype(F32), level1)
    level2 = (chip_out[:, :rank].astype(F32) + z_in[:, :rank].astype(F32)).astype(BF)
    chip_copy[1].wait_recv()
    chip_copy[2].wait_recv()
    weigh(2, y_in[...].astype(F32) + yz_in[...].astype(F32), level2)
    e_out[...] = mdot(far[...], stack[...]).astype(BF)
    e_core_copy = send(e_out.at[far_half, :], e_core, "core")

    near_part(0, feat_in[0, :, :rows])

    e_core_copy.wait_recv()
    for copy in r_x_copy:
        copy.wait_recv()
    g_half[...] = (r_x[0].astype(F32) + r_x[1].astype(F32)
                   - (e_out[near_half, :].astype(F32) + e_core[...].astype(F32)))
    g_part[...] = g_half[far_quarter, :].astype(BF)
    g_y_copy = send(g_part, g_y, "y")

    near_part(2, feat_in[1, :, :rows])

    g_y_copy.wait_recv()
    g_own[...] = g_half[near_quarter, :] + g_y[...].astype(F32)
    g_out[...] = g_own[...].astype(BF)
    g_z_copy = send(g_out, g_z, "z")

    def spread(total, result, t_out, t_y):
        result[top_quarter, :] = total
        t_out[...] = total.astype(BF)
        place = result.at[top_quarter, :]
        return send(t_out, t_y, "y"), send(place, place, "core")

    def collect(copies, result, t_y, t_core):
        copies[0].wait_recv()
        last = send(t_y, t_core, "core")
        result[quarter_of(bits[0], 1 - bits[2]), :] = t_y[...].astype(F32)
        return last

    def finish(copies, last, result, t_core):
        copies[1].wait_recv()
        last.wait_recv()
        result[quarter_of(1 - bits[0], 1 - bits[2]), :] = t_core[...].astype(F32)

    def block_rows_sum(chunks, start, size):
        at = slice(start, start + size)
        for j in chunks:
            for copy in stream[j]:
                copy.wait_recv()
        sample[:, at] = mdot(near[...], wide[:, at]).astype(BF)

    o_z_copy.wait_recv()
    o_spread = spread(o_q[...] + o_z[...].astype(F32), omega, o_t, o_ty)
    block_rows_sum((0, 1), 0, cols // 2)
    o_last = collect(o_spread, omega, o_ty, o_tc)

    g_z_copy.wait_recv()
    g_spread = spread(g_own[...] + g_z[...].astype(F32), top, g_t, g_ty)
    finish(o_spread, o_last, omega, o_tc)
    g_last = collect(g_spread, top, g_ty, g_tc)

    block_rows_sum((2,), cols // 2, cols // 2)
    finish(g_spread, g_last, top, g_tc)
    for copy in pending:
        copy.wait_send()


def write_out(a, b, c, a_out, b_out, c_out, sem):
    copies = [pltpu.make_async_copy(src, dst, sem.at[i])
              for i, (src, dst) in enumerate(((a, a_out), (b, b_out), (c, c_out)))]
    for copy in copies:
        copy.start()
    for copy in copies:
        copy.wait()


def on_device(n_blk, points, test_matrix, near_lists, leaf_pivots, leaf_proj, merge_pivots, merge_proj):
    rows, cols = test_matrix.shape
    rank = leaf_pivots.shape[1]
    slots = near_lists.shape[1]
    near_amp = 9.0 / math.sqrt(slots * (rows // near_lists.shape[0]))
    far_amp = 3.0 / math.sqrt(rank)
    half = rank // 2
    quarter = rank // 4
    vmem = pl.BlockSpec(memory_space=pltpu.VMEM)
    hbm = pl.BlockSpec(memory_space=pltpu.HBM)
    anyw = pl.BlockSpec(memory_space=pl.ANY)
    copies = 28
    scratch = [
        pltpu.VMEM(near_lists.shape, jnp.int32),
        pltpu.VMEM(points.shape, BF),
        pltpu.VMEM(leaf_pivots.shape, jnp.int32),
        pltpu.VMEM(merge_pivots.shape, jnp.int32),
        pltpu.VMEM(leaf_proj.shape, BF),
        pltpu.VMEM(merge_proj.shape, BF),
        pltpu.VMEM((3 * rows, cols), BF),
        pltpu.VMEM((3 * rank, cols), BF),
        pltpu.VMEM((rows, 3 * rows), BF),
        pltpu.VMEM((rank, 3 * rank), BF),
        pltpu.VMEM((16, rows + rank), BF),
        pltpu.VMEM((2, 16, rows + rank), BF),
        pltpu.VMEM((16, 3 * rank), BF),
        pltpu.VMEM((16, 3 * rank), BF),
        pltpu.VMEM((16, 2 * rank), BF),
        pltpu.VMEM((16, 2 * rank), BF),
        pltpu.VMEM((16, rank), BF),
        pltpu.VMEM((16, rank), BF),
        pltpu.VMEM((rank, cols), F32),
        pltpu.VMEM((half, cols), F32),
        pltpu.VMEM((half, cols), F32),
        pltpu.VMEM((quarter, cols), F32),
    ] + [pltpu.VMEM((quarter, cols), BF)] * 7 + [
        pltpu.VMEM((2, rank, cols), BF),
        pltpu.VMEM((2, half, cols), BF),
        pltpu.VMEM((2, half, cols), BF),
        pltpu.VMEM((2, half, cols), BF),
        pltpu.VMEM((rank, cols), BF),
        pltpu.VMEM((half, cols), BF),
        pltpu.VMEM((half, cols), F32),
        pltpu.VMEM((quarter, cols), F32),
    ] + [pltpu.VMEM((quarter, cols), BF)] * 7 + [
        pltpu.SemaphoreType.DMA((7,)),
        pltpu.SemaphoreType.DMA((copies,)),
        pltpu.SemaphoreType.DMA((copies,)),
    ]
    shapes = (
        jax.ShapeDtypeStruct((rows, cols), BF),
        jax.ShapeDtypeStruct((rank, cols), F32),
        jax.ShapeDtypeStruct((rank, cols), F32),
    )
    operands = [
        pltpu.with_memory_space_constraint(v, pltpu.HBM)
        for v in (near_lists, points, leaf_pivots, merge_pivots, test_matrix, leaf_proj, merge_proj)
    ]
    made = pl.pallas_call(
        functools.partial(body, n_blk, near_amp, far_amp),
        name="hss",
        out_shape=shapes,
        in_specs=[hbm] * 7,
        out_specs=(vmem, vmem, vmem),
        scratch_shapes=scratch,
        compiler_params=pltpu.CompilerParams(
            collective_id=0, has_side_effects=True, vmem_limit_bytes=40 << 20),
    )(*operands)
    return pl.pallas_call(
        write_out,
        name="write_out",
        out_shape=shapes,
        in_specs=[anyw] * 3,
        out_specs=(anyw, anyw, anyw),
        scratch_shapes=[pltpu.SemaphoreType.DMA((3,))],
        compiler_params=pltpu.CompilerParams(vmem_limit_bytes=1 << 20),
    )(*made)


def solution(mesh):
    placed = (
        P(None, ("blk", "leaf")),
        P(("blk", "leaf"), None),
        P(("blk", "leaf"), None),
        P(("blk", "leaf"), None),
        P(("blk", "leaf"), None),
        P(None, ("blk", "leaf"), None),
        P(None, ("blk", "leaf"), None, None),
    )
    return jax.shard_map(
        functools.partial(on_device, mesh.shape["blk"]),
        mesh=mesh,
        in_specs=placed,
        out_specs=(P(("blk", "leaf"), None), P(("blk", "leaf"), None), P(("blk", "leaf"), None)),
        check_vma=False,
    )
```

```python
import functools
import math

import jax
import jax.numpy as jnp
from jax import lax
from jax.experimental import pallas as pl
from jax.experimental.pallas import tpu as pltpu
from jax.sharding import PartitionSpec as P

SPREAD = 25.0
MESH = pl.DeviceIdType.MESH
BF = jnp.bfloat16
F32 = jnp.float32
FAR = -512.0
SCALE = 2.0 * SPREAD / math.log(2.0)


def tdot(a, b):
    return lax.dot_general(a, b, (((0,), (0,)), ((), ())), preferred_element_type=F32)


def mdot(a, b):
    return jnp.dot(a, b, preferred_element_type=F32)


def rows_of(shape, entries):
    index = lax.broadcasted_iota(jnp.int32, shape, 0)
    result = jnp.zeros(shape, F32)
    for at, value in entries:
        result = jnp.where(index == at, value, result)
    return result


PLACES = ((9, 10), (14, 15), (12, 13))


def features(points, lists, block_rows):
    count = points.shape[1]
    x, y, z = points[0:1], points[1:2], points[2:3]
    half = 0.5 * (x * x + y * y + z * z)
    high = half.astype(BF).astype(F32)
    mid = (half - high).astype(BF).astype(F32)
    low = (half - high - mid).astype(BF).astype(F32)
    lane = lax.broadcasted_iota(jnp.int32, (1, count), 1)
    entries = [(0, x), (1, y), (2, z), (3, 1.0), (4, 1.0), (5, 1.0), (6, high), (7, mid), (8, low)]
    for place, at in enumerate(PLACES):
        for j in range(2):
            listed = jnp.max((lists == 2 * place + j).astype(F32), axis=1, keepdims=True)
            skipped = (1.0 - listed) * FAR
            entries.append((at[j], jnp.where(lane < block_rows, skipped[0:1], skipped[1:2])))
    return rows_of((16, count), entries)


def source_side(feat, place=None):
    r = lax.broadcasted_iota(jnp.int32, (16, 16), 0)
    c = lax.broadcasted_iota(jnp.int32, (16, 16), 1)
    same = (r == c) & (r < 3)
    swap = ((r >= 3) & (r < 6) & (c == r + 3)) | ((r >= 6) & (r < 9) & (c == r - 3))
    form = jnp.where(same, 1.0, jnp.where(swap, -1.0, 0.0)).astype(BF)
    turned = mdot(form, feat)
    count = feat.shape[1]
    extra = [(11, FAR)]
    if place is not None:
        lane = lax.broadcasted_iota(jnp.int32, (1, count), 1)
        first = (lane < count // 2).astype(F32)
        extra += [(PLACES[place][0], first), (PLACES[place][1], 1.0 - first)]
    return (turned + rows_of(turned.shape, extra)).astype(BF)


def only_valid(feat):
    index = lax.broadcasted_iota(jnp.int32, feat.shape, 0)
    return jnp.where(index == 11, 1.0 - feat[3:4], feat).astype(BF)


def kernel_of(target, source, amp):
    return jnp.exp2(tdot(target, source) * SCALE + math.log2(amp))


def one_hot(pivots, offset, count):
    k = lax.broadcasted_iota(jnp.int32, (count, pivots.shape[1]), 0)
    return jnp.where(k == pivots - offset, 1.0, 0.0).astype(BF)


def body(n_blk, near_amp, far_amp,
         lists_hbm, points_hbm, pivots_hbm, tree_pivots_hbm, test_hbm, proj_hbm, tree_hbm,
         sample, top, omega,
         lists, points, pivots, tree_pivots, proj, tree, wide, stack, near, far,
         feat_out, feat_in, kept_out, kept_in, chip_out, z_in, y_in, yz_in,
         o_out, o_core, o_sum, o_q, o_part, o_y, o_send, o_z, o_t, o_ty, o_tc,
         r_out, r_core, r_sum, r_x, e_out, e_core, g_half, g_own,
         g_part, g_y, g_out, g_z, t_out, t_y, t_core,
         hello, local_sem, send_sem, recv_sem):
    b = lax.axis_index("blk")
    l = lax.axis_index("leaf")
    bits = [lax.rem(l // (1 << t), 2) for t in range(3)]
    step = [(1 << t) - (2 << t) * bits[t] for t in range(3)]
    peers = {
        "next": {"blk": lax.rem(b + 1, n_blk), "leaf": l},
        "prev": {"blk": lax.rem(b + n_blk - 1, n_blk), "leaf": l},
        "core": {"blk": b, "leaf": l + step[0]},
        "z": {"blk": b, "leaf": l + step[1]},
        "y": {"blk": b, "leaf": l + step[2]},
        "yz": {"blk": b, "leaf": l + step[1] + step[2]},
    }
    barrier = pltpu.get_barrier_semaphore()
    upper = bits[1]
    for name in ("next", "prev", "core", "y"):
        pl.semaphore_signal(barrier, inc=1, device_id=peers[name], device_id_type=MESH)

    @pl.when(upper == 0)
    def _():
        for name in ("z", "yz"):
            pl.semaphore_signal(barrier, inc=1, device_id=peers[name], device_id_type=MESH)

    rows, rank = proj.shape
    block_rows = rows // 2
    half = rank // 2
    quarter = half // 2
    pending = []

    def plan(src, dst, peer):
        at = len(pending)
        copy = pltpu.make_async_remote_copy(
            src_ref=src, dst_ref=dst, send_sem=send_sem.at[at], recv_sem=recv_sem.at[at],
            device_id=peers[peer], device_id_type=MESH)
        pending.append(copy)
        return copy

    def send(src, dst, peer):
        copy = plan(src, dst, peer)
        copy.start()
        return copy

    def fetch(at, src, dst):
        copy = pltpu.make_async_copy(src, dst, local_sem.at[at])
        copy.start()
        return copy

    small = [fetch(0, lists_hbm, lists), fetch(1, points_hbm, points),
             fetch(2, pivots_hbm, pivots), fetch(3, tree_pivots_hbm, tree_pivots)]
    large = [fetch(4, test_hbm, wide.at[pl.ds(rows, rows), :]), fetch(5, proj_hbm, proj),
             fetch(6, tree_hbm, tree)]

    near_half = pl.ds(pl.multiple_of(bits[0] * half, half), half)
    far_half = pl.ds(pl.multiple_of((1 - bits[0]) * half, half), half)
    near_quarter = pl.ds(pl.multiple_of(bits[2] * quarter, quarter), quarter)
    far_quarter = pl.ds(pl.multiple_of((1 - bits[2]) * quarter, quarter), quarter)

    def quarter_of(core, part):
        return pl.ds(pl.multiple_of(core * half + part * quarter, quarter), quarter)

    top_quarter = quarter_of(bits[0], bits[2])

    for copy in small:
        copy.wait()
    own = features(points[...].astype(F32), lists[...], block_rows).astype(BF)
    skeleton = mdot(own, one_hot(pivots[...], 0, rows)).astype(BF)
    kept = skeleton
    for t in range(3):
        kept = mdot(kept, one_hot(tree_pivots[t], rank * bits[t], rank)).astype(BF)
        kept_out[:, t * rank:(t + 1) * rank] = kept
    feat_out[:, :rows] = own
    feat_out[:, rows:] = only_valid(kept.astype(F32))

    @pl.when(upper == 0)
    def _():
        pl.semaphore_wait(barrier, 4)

    @pl.when(upper == 1)
    def _():
        pl.semaphore_wait(barrier, 6)
        for at, name in enumerate(("z", "yz")):
            pl.semaphore_signal(hello.at[at], inc=1, device_id=peers[name], device_id_type=MESH)

    feat_copy = [send(feat_out, feat_in.at[0], "next"), send(feat_out, feat_in.at[1], "prev")]
    kept_copy = send(kept_out, kept_in, "core")

    cols = wide.shape[1]
    wing = cols // 2
    wings = [pl.ds(h * wing, wing) for h in range(2)]
    cut = [slice(h * wing, (h + 1) * wing) for h in range(2)]

    def stream_chunk(start, size):
        at = pl.ds(start, size)
        return [
            send(test_hbm.at[:, at], wide.at[pl.ds(0, rows), at], "next"),
            send(test_hbm.at[:, at], wide.at[pl.ds(2 * rows, rows), at], "prev"),
        ]

    stream = [stream_chunk(0, wing)]

    kept_copy.wait_recv()
    chip = kept_out[...].astype(F32) + kept_in[...].astype(F32)
    level1 = chip[:, :rank].astype(BF)
    chip_out[...] = chip[:, rank:].astype(BF)
    last_rank = pl.ds(rank, rank)
    chip_copy = [
        plan(chip_out, z_in, "z"),
        plan(chip_out.at[:, last_rank], yz_in, "yz"),
        send(chip_out.at[:, last_rank], y_in, "y"),
    ]

    @pl.when(upper == 1)
    def _():
        for copy in chip_copy[:2]:
            copy.start()

    for copy in large:
        copy.wait()

    r_core_copy = []
    for side, place in ((0, 2), (1, 0)):
        feat_copy[side].wait_recv()
        weights = kernel_of(feat_in[side, :, rows:], source_side(own, place), near_amp).astype(BF)
        r_out[side] = mdot(weights, wide[rows:2 * rows, :]).astype(BF)
        r_core_copy.append(send(r_out.at[side, far_half, :], r_core.at[side], "core"))

    share = tdot(proj[...], wide[rows:2 * rows, :])
    for t in range(3):
        high = share.astype(BF)
        low = (share - high.astype(F32)).astype(BF)
        stack[t * rank:(t + 1) * rank, :] = high
        child = tree[t, 0, pl.ds(pl.multiple_of(rank * bits[t], rank), rank), :]
        share = tdot(child, high) + tdot(child, low)
    o_out[...] = share

    r_x_copy = [[], []]
    for side, name in ((0, "prev"), (1, "next")):
        r_core_copy[side].wait_recv()
        r_sum[side] = (r_out[side, near_half, :].astype(F32) + r_core[side].astype(F32)).astype(BF)
        for h, at in enumerate(wings):
            r_x_copy[h].append(send(r_sum.at[side, :, at], r_x.at[1 - side, :, at], name))
    o_core_copy = send(o_out.at[far_half, :], o_core, "core")

    def weigh(t, feat, source):
        at = slice(t * rank, (t + 1) * rank)
        far[:, at] = kernel_of(only_valid(feat), source_side(source), far_amp).astype(BF)

    def near_part(place, feat):
        at = slice(place * rows, (place + 1) * rows)
        near[:, at] = kernel_of(own, source_side(feat, place), near_amp).astype(BF)

    weigh(0, kept_in[:, 2 * rank:].astype(F32), skeleton)
    near_part(1, own)

    o_core_copy.wait_recv()
    o_sum[...] = o_out[near_half, :] + o_core[...]
    o_part[...] = o_sum[far_quarter, :].astype(BF)
    o_y_copy = send(o_part, o_y, "y")

    @pl.when(upper == 0)
    def _():
        for at in range(2):
            pl.semaphore_wait(hello.at[at], 1)
        for copy in chip_copy[:2]:
            copy.start()

    near_part(0, feat_in[0, :, :rows])

    for copy in chip_copy:
        copy.wait_recv()
    weigh(1, z_in[:, rank:].astype(F32), level1)
    level2 = (chip_out[:, :rank].astype(F32) + z_in[:, :rank].astype(F32)).astype(BF)
    weigh(2, y_in[...].astype(F32) + yz_in[...].astype(F32), level2)
    e_out[...] = mdot(far[...], stack[...]).astype(BF)
    e_core_copy = send(e_out.at[far_half, :], e_core, "core")
    o_y_copy.wait_recv()
    o_q[...] = o_sum[near_quarter, :] + o_y[...].astype(F32)
    o_send[...] = o_q[...].astype(BF)
    o_z_copy = send(o_send, o_z, "z")

    g_y_copy, g_z_copy, t_y_copy, t_core_copy, t_last = {}, {}, {}, {}, {}

    def y_stage(h):
        at = cut[h]
        for copy in r_x_copy[h]:
            copy.wait_recv()
        g_half[:, at] = r_x[0, :, at].astype(F32) + r_x[1, :, at].astype(F32) - g_half[:, at]
        g_part[:, at] = g_half[far_quarter, at].astype(BF)
        g_y_copy[h] = send(g_part.at[:, wings[h]], g_y.at[:, wings[h]], "y")

    def z_stage(h):
        at = cut[h]
        g_y_copy[h].wait_recv()
        g_own[:, at] = g_half[near_quarter, at] + g_y[:, at].astype(F32)
        g_out[:, at] = g_own[:, at].astype(BF)
        g_z_copy[h] = send(g_out.at[:, wings[h]], g_z.at[:, wings[h]], "z")

    def top_stage(h):
        at = cut[h]
        g_z_copy[h].wait_recv()
        total = g_own[:, at] + g_z[:, at].astype(F32)
        top[top_quarter, at] = total
        t_out[:, at] = total.astype(BF)
        t_y_copy[h] = send(t_out.at[:, wings[h]], t_y.at[:, wings[h]], "y")
        place = top.at[top_quarter, wings[h]]
        t_core_copy[h] = send(place, place, "core")

    def last_stage(h):
        at = cut[h]
        t_y_copy[h].wait_recv()
        t_last[h] = send(t_y.at[:, wings[h]], t_core.at[:, wings[h]], "core")
        top[quarter_of(bits[0], 1 - bits[2]), at] = t_y[:, at].astype(F32)

    def block_rows_sum(h):
        for copy in stream[h]:
            copy.wait_recv()
        sample[:, cut[h]] = mdot(near[...], wide[:, cut[h]]).astype(BF)

    e_core_copy.wait_recv()
    g_half[...] = e_out[near_half, :].astype(F32) + e_core[...].astype(F32)
    y_stage(0)
    y_stage(1)
    z_stage(0)
    z_stage(1)
    stream.append(stream_chunk(wing, wing))

    near_part(2, feat_in[1, :, :rows])
    block_rows_sum(0)

    top_stage(0)
    top_stage(1)
    o_z_copy.wait_recv()
    total = o_q[...] + o_z[...].astype(F32)
    omega[top_quarter, :] = total
    o_t[...] = total.astype(BF)
    o_t_copy = send(o_t, o_ty, "y")
    place = omega.at[top_quarter, :]
    o_own_copy = send(place, place, "core")
    last_stage(0)
    last_stage(1)
    o_t_copy.wait_recv()
    o_last = send(o_ty, o_tc, "core")
    omega[quarter_of(bits[0], 1 - bits[2]), :] = o_ty[...].astype(F32)
    block_rows_sum(1)

    other = quarter_of(1 - bits[0], 1 - bits[2])
    for h in range(2):
        t_core_copy[h].wait_recv()
        t_last[h].wait_recv()
    top[other, :] = t_core[...].astype(F32)
    o_own_copy.wait_recv()
    o_last.wait_recv()
    omega[other, :] = o_tc[...].astype(F32)
    for copy in pending:
        copy.wait_send()


def write_out(a, b, c, a_out, b_out, c_out, sem):
    copies = [pltpu.make_async_copy(src, dst, sem.at[i])
              for i, (src, dst) in enumerate(((a, a_out), (b, b_out), (c, c_out)))]
    for copy in copies:
        copy.start()
    for copy in copies:
        copy.wait()


def on_device(n_blk, points, test_matrix, near_lists, leaf_pivots, leaf_proj, merge_pivots, merge_proj):
    rows, cols = test_matrix.shape
    rank = leaf_pivots.shape[1]
    slots = near_lists.shape[1]
    near_amp = 9.0 / math.sqrt(slots * (rows // near_lists.shape[0]))
    far_amp = 3.0 / math.sqrt(rank)
    half = rank // 2
    quarter = rank // 4
    vmem = pl.BlockSpec(memory_space=pltpu.VMEM)
    hbm = pl.BlockSpec(memory_space=pltpu.HBM)
    anyw = pl.BlockSpec(memory_space=pl.ANY)
    copies = 40
    scratch = [
        pltpu.VMEM(near_lists.shape, jnp.int32),
        pltpu.VMEM(points.shape, BF),
        pltpu.VMEM(leaf_pivots.shape, jnp.int32),
        pltpu.VMEM(merge_pivots.shape, jnp.int32),
        pltpu.VMEM(leaf_proj.shape, BF),
        pltpu.VMEM(merge_proj.shape, BF),
        pltpu.VMEM((3 * rows, cols), BF),
        pltpu.VMEM((3 * rank, cols), BF),
        pltpu.VMEM((rows, 3 * rows), BF),
        pltpu.VMEM((rank, 3 * rank), BF),
        pltpu.VMEM((16, rows + rank), BF),
        pltpu.VMEM((2, 16, rows + rank), BF),
        pltpu.VMEM((16, 3 * rank), BF),
        pltpu.VMEM((16, 3 * rank), BF),
        pltpu.VMEM((16, 2 * rank), BF),
        pltpu.VMEM((16, 2 * rank), BF),
        pltpu.VMEM((16, rank), BF),
        pltpu.VMEM((16, rank), BF),
        pltpu.VMEM((rank, cols), F32),
        pltpu.VMEM((half, cols), F32),
        pltpu.VMEM((half, cols), F32),
        pltpu.VMEM((quarter, cols), F32),
    ] + [pltpu.VMEM((quarter, cols), BF)] * 7 + [
        pltpu.VMEM((2, rank, cols), BF),
        pltpu.VMEM((2, half, cols), BF),
        pltpu.VMEM((2, half, cols), BF),
        pltpu.VMEM((2, half, cols), BF),
        pltpu.VMEM((rank, cols), BF),
        pltpu.VMEM((half, cols), BF),
        pltpu.VMEM((half, cols), F32),
        pltpu.VMEM((quarter, cols), F32),
    ] + [pltpu.VMEM((quarter, cols), BF)] * 7 + [
        pltpu.SemaphoreType.REGULAR((2,)),
        pltpu.SemaphoreType.DMA((7,)),
        pltpu.SemaphoreType.DMA((copies,)),
        pltpu.SemaphoreType.DMA((copies,)),
    ]
    shapes = (
        jax.ShapeDtypeStruct((rows, cols), BF),
        jax.ShapeDtypeStruct((rank, cols), F32),
        jax.ShapeDtypeStruct((rank, cols), F32),
    )
    operands = [
        pltpu.with_memory_space_constraint(v, pltpu.HBM)
        for v in (near_lists, points, leaf_pivots, merge_pivots, test_matrix, leaf_proj, merge_proj)
    ]
    made = pl.pallas_call(
        functools.partial(body, n_blk, near_amp, far_amp),
        name="hss",
        out_shape=shapes,
        in_specs=[hbm] * 7,
        out_specs=(vmem, vmem, vmem),
        scratch_shapes=scratch,
        compiler_params=pltpu.CompilerParams(
            collective_id=0, has_side_effects=True, vmem_limit_bytes=40 << 20),
    )(*operands)
    return pl.pallas_call(
        write_out,
        name="write_out",
        out_shape=shapes,
        in_specs=[anyw] * 3,
        out_specs=(anyw, anyw, anyw),
        scratch_shapes=[pltpu.SemaphoreType.DMA((3,))],
        compiler_params=pltpu.CompilerParams(vmem_limit_bytes=1 << 20),
    )(*made)


def solution(mesh):
    placed = (
        P(None, ("blk", "leaf")),
        P(("blk", "leaf"), None),
        P(("blk", "leaf"), None),
        P(("blk", "leaf"), None),
        P(("blk", "leaf"), None),
        P(None, ("blk", "leaf"), None),
        P(None, ("blk", "leaf"), None, None),
    )
    return jax.shard_map(
        functools.partial(on_device, mesh.shape["blk"]),
        mesh=mesh,
        in_specs=placed,
        out_specs=(P(("blk", "leaf"), None), P(("blk", "leaf"), None), P(("blk", "leaf"), None)),
        check_vma=False,
    )
```

```python
import functools
import math

import jax
import jax.numpy as jnp
from jax import lax
from jax.experimental import pallas as pl
from jax.experimental.pallas import tpu as pltpu
from jax.sharding import PartitionSpec as P

SPREAD = 25.0
MESH = pl.DeviceIdType.MESH
BF = jnp.bfloat16
F32 = jnp.float32
FAR = -512.0
SCALE = 2.0 * SPREAD / math.log(2.0)


def tdot(a, b):
    return lax.dot_general(a, b, (((0,), (0,)), ((), ())), preferred_element_type=F32)


def mdot(a, b):
    return jnp.dot(a, b, preferred_element_type=F32)


def rows_of(shape, entries):
    index = lax.broadcasted_iota(jnp.int32, shape, 0)
    result = jnp.zeros(shape, F32)
    for at, value in entries:
        result = jnp.where(index == at, value, result)
    return result


PLACES = ((9, 10), (14, 15), (12, 13))


def features(points, lists, block_rows):
    count = points.shape[1]
    x, y, z = points[0:1], points[1:2], points[2:3]
    half = 0.5 * (x * x + y * y + z * z)
    high = half.astype(BF).astype(F32)
    mid = (half - high).astype(BF).astype(F32)
    low = (half - high - mid).astype(BF).astype(F32)
    lane = lax.broadcasted_iota(jnp.int32, (1, count), 1)
    entries = [(0, x), (1, y), (2, z), (3, 1.0), (4, 1.0), (5, 1.0), (6, high), (7, mid), (8, low)]
    for place, at in enumerate(PLACES):
        for j in range(2):
            listed = jnp.max((lists == 2 * place + j).astype(F32), axis=1, keepdims=True)
            skipped = (1.0 - listed) * FAR
            entries.append((at[j], jnp.where(lane < block_rows, skipped[0:1], skipped[1:2])))
    return rows_of((16, count), entries)


def source_side(feat, place=None):
    r = lax.broadcasted_iota(jnp.int32, (16, 16), 0)
    c = lax.broadcasted_iota(jnp.int32, (16, 16), 1)
    same = (r == c) & (r < 3)
    swap = ((r >= 3) & (r < 6) & (c == r + 3)) | ((r >= 6) & (r < 9) & (c == r - 3))
    form = jnp.where(same, 1.0, jnp.where(swap, -1.0, 0.0)).astype(BF)
    turned = mdot(form, feat)
    count = feat.shape[1]
    extra = [(11, FAR)]
    if place is not None:
        lane = lax.broadcasted_iota(jnp.int32, (1, count), 1)
        first = (lane < count // 2).astype(F32)
        extra += [(PLACES[place][0], first), (PLACES[place][1], 1.0 - first)]
    return (turned + rows_of(turned.shape, extra)).astype(BF)


def only_valid(feat):
    index = lax.broadcasted_iota(jnp.int32, feat.shape, 0)
    return jnp.where(index == 11, 1.0 - feat[3:4], feat).astype(BF)


def kernel_of(target, source, amp):
    return jnp.exp2(tdot(target, source) * SCALE + math.log2(amp))


def one_hot(pivots, offset, count):
    k = lax.broadcasted_iota(jnp.int32, (count, pivots.shape[1]), 0)
    return jnp.where(k == pivots - offset, 1.0, 0.0).astype(BF)


def body(n_blk, near_amp, far_amp,
         lists_hbm, points_hbm, pivots_hbm, tree_pivots_hbm, test_hbm, proj_hbm, tree_hbm,
         sample, top, omega,
         lists, points, pivots, tree_pivots, proj, tree, wide, stack, near, far,
         feat_out, feat_in, kept_out, kept_in, chip_out, z_in, y_in, yz_in,
         o_out, o_core, o_sum, o_q, o_part, o_y, o_send, o_z, o_t, o_ty, o_tc,
         r_out, r_core, r_sum, r_x, e_out, e_core, g_half, g_own,
         g_part, g_y, g_out, g_z, t_out, t_y, t_core,
         hello, local_sem, send_sem, recv_sem):
    b = lax.axis_index("blk")
    l = lax.axis_index("leaf")
    bits = [lax.rem(l // (1 << t), 2) for t in range(3)]
    step = [(1 << t) - (2 << t) * bits[t] for t in range(3)]
    peers = {
        "next": {"blk": lax.rem(b + 1, n_blk), "leaf": l},
        "prev": {"blk": lax.rem(b + n_blk - 1, n_blk), "leaf": l},
        "core": {"blk": b, "leaf": l + step[0]},
        "z": {"blk": b, "leaf": l + step[1]},
        "y": {"blk": b, "leaf": l + step[2]},
        "yz": {"blk": b, "leaf": l + step[1] + step[2]},
    }
    barrier = pltpu.get_barrier_semaphore()
    upper = bits[1]
    for name in ("next", "prev", "core", "y"):
        pl.semaphore_signal(barrier, inc=1, device_id=peers[name], device_id_type=MESH)

    @pl.when(upper == 0)
    def _():
        for name in ("z", "yz"):
            pl.semaphore_signal(barrier, inc=1, device_id=peers[name], device_id_type=MESH)

    rows, rank = proj.shape
    block_rows = rows // 2
    half = rank // 2
    quarter = half // 2
    pending = []

    def plan(src, dst, peer):
        at = len(pending)
        copy = pltpu.make_async_remote_copy(
            src_ref=src, dst_ref=dst, send_sem=send_sem.at[at], recv_sem=recv_sem.at[at],
            device_id=peers[peer], device_id_type=MESH)
        pending.append(copy)
        return copy

    def send(src, dst, peer):
        copy = plan(src, dst, peer)
        copy.start()
        return copy

    def fetch(at, src, dst):
        copy = pltpu.make_async_copy(src, dst, local_sem.at[at])
        copy.start()
        return copy

    small = [fetch(0, lists_hbm, lists), fetch(1, points_hbm, points),
             fetch(2, pivots_hbm, pivots), fetch(3, tree_pivots_hbm, tree_pivots)]
    large = [fetch(4, test_hbm, wide.at[pl.ds(rows, rows), :]), fetch(5, proj_hbm, proj),
             fetch(6, tree_hbm, tree)]

    near_half = pl.ds(pl.multiple_of(bits[0] * half, half), half)
    far_half = pl.ds(pl.multiple_of((1 - bits[0]) * half, half), half)
    near_quarter = pl.ds(pl.multiple_of(bits[2] * quarter, quarter), quarter)
    far_quarter = pl.ds(pl.multiple_of((1 - bits[2]) * quarter, quarter), quarter)

    def quarter_of(core, part):
        return pl.ds(pl.multiple_of(core * half + part * quarter, quarter), quarter)

    top_quarter = quarter_of(bits[0], bits[2])

    for copy in small:
        copy.wait()
    own = features(points[...].astype(F32), lists[...], block_rows).astype(BF)
    skeleton = mdot(own, one_hot(pivots[...], 0, rows)).astype(BF)
    kept = skeleton
    for t in range(3):
        kept = mdot(kept, one_hot(tree_pivots[t], rank * bits[t], rank)).astype(BF)
        kept_out[:, t * rank:(t + 1) * rank] = kept
    feat_out[:, :rows] = own
    feat_out[:, rows:] = only_valid(kept.astype(F32))

    @pl.when(upper == 0)
    def _():
        pl.semaphore_wait(barrier, 4)

    @pl.when(upper == 1)
    def _():
        pl.semaphore_wait(barrier, 6)
        for at, name in enumerate(("z", "yz")):
            pl.semaphore_signal(hello.at[at], inc=1, device_id=peers[name], device_id_type=MESH)

    feat_copy = [send(feat_out, feat_in.at[0], "next"), send(feat_out, feat_in.at[1], "prev")]
    kept_copy = send(kept_out, kept_in, "core")

    cols = wide.shape[1]
    wing = cols // 2
    wings = [pl.ds(h * wing, wing) for h in range(2)]
    cut = [slice(h * wing, (h + 1) * wing) for h in range(2)]

    def stream_chunk(start, size):
        at = pl.ds(start, size)
        return [
            send(test_hbm.at[:, at], wide.at[pl.ds(0, rows), at], "next"),
            send(test_hbm.at[:, at], wide.at[pl.ds(2 * rows, rows), at], "prev"),
        ]

    stream = [stream_chunk(0, wing // 2)]

    kept_copy.wait_recv()
    chip = kept_out[...].astype(F32) + kept_in[...].astype(F32)
    level1 = chip[:, :rank].astype(BF)
    chip_out[...] = chip[:, rank:].astype(BF)
    last_rank = pl.ds(rank, rank)
    chip_copy = [
        plan(chip_out, z_in, "z"),
        plan(chip_out.at[:, last_rank], yz_in, "yz"),
        send(chip_out.at[:, last_rank], y_in, "y"),
    ]

    @pl.when(upper == 1)
    def _():
        for copy in chip_copy[:2]:
            copy.start()

    for copy in large:
        copy.wait()

    r_core_copy = []
    for side, place in ((0, 2), (1, 0)):
        feat_copy[side].wait_recv()
        weights = kernel_of(feat_in[side, :, rows:], source_side(own, place), near_amp).astype(BF)
        r_out[side] = mdot(weights, wide[rows:2 * rows, :]).astype(BF)
        r_core_copy.append(send(r_out.at[side, far_half, :], r_core.at[side], "core"))

    share = tdot(proj[...], wide[rows:2 * rows, :])
    for t in range(3):
        high = share.astype(BF)
        low = (share - high.astype(F32)).astype(BF)
        stack[t * rank:(t + 1) * rank, :] = high
        child = tree[t, 0, pl.ds(pl.multiple_of(rank * bits[t], rank), rank), :]
        share = tdot(child, high) + tdot(child, low)
    o_out[...] = share

    r_x_copy = [[], []]
    for side, name in ((0, "prev"), (1, "next")):
        r_core_copy[side].wait_recv()
        r_sum[side] = (r_out[side, near_half, :].astype(F32) + r_core[side].astype(F32)).astype(BF)
        for h, at in enumerate(wings):
            r_x_copy[h].append(send(r_sum.at[side, :, at], r_x.at[1 - side, :, at], name))
    o_core_copy = send(o_out.at[far_half, :], o_core, "core")

    def weigh(t, feat, source):
        at = slice(t * rank, (t + 1) * rank)
        far[:, at] = kernel_of(only_valid(feat), source_side(source), far_amp).astype(BF)

    def near_part(place, feat):
        at = slice(place * rows, (place + 1) * rows)
        near[:, at] = kernel_of(own, source_side(feat, place), near_amp).astype(BF)

    weigh(0, kept_in[:, 2 * rank:].astype(F32), skeleton)
    near_part(1, own)

    o_core_copy.wait_recv()
    o_sum[...] = o_out[near_half, :] + o_core[...]
    o_part[...] = o_sum[far_quarter, :].astype(BF)
    o_y_copy = send(o_part, o_y, "y")

    @pl.when(upper == 0)
    def _():
        for at in range(2):
            pl.semaphore_wait(hello.at[at], 1)
        for copy in chip_copy[:2]:
            copy.start()

    near_part(0, feat_in[0, :, :rows])

    for copy in chip_copy:
        copy.wait_recv()
    weigh(1, z_in[:, rank:].astype(F32), level1)
    level2 = (chip_out[:, :rank].astype(F32) + z_in[:, :rank].astype(F32)).astype(BF)
    weigh(2, y_in[...].astype(F32) + yz_in[...].astype(F32), level2)
    e_out[...] = mdot(far[...], stack[...]).astype(BF)
    e_core_copy = send(e_out.at[far_half, :], e_core, "core")
    o_y_copy.wait_recv()
    o_q[...] = o_sum[near_quarter, :] + o_y[...].astype(F32)
    o_send[...] = o_q[...].astype(BF)
    o_z_copy = send(o_send, o_z, "z")

    g_y_copy, g_z_copy, t_y_copy, t_core_copy, t_last = {}, {}, {}, {}, {}

    def y_stage(h):
        at = cut[h]
        for copy in r_x_copy[h]:
            copy.wait_recv()
        g_half[:, at] = r_x[0, :, at].astype(F32) + r_x[1, :, at].astype(F32) - g_half[:, at]
        g_part[:, at] = g_half[far_quarter, at].astype(BF)
        g_y_copy[h] = send(g_part.at[:, wings[h]], g_y.at[:, wings[h]], "y")

    def z_stage(h):
        at = cut[h]
        g_y_copy[h].wait_recv()
        g_own[:, at] = g_half[near_quarter, at] + g_y[:, at].astype(F32)
        g_out[:, at] = g_own[:, at].astype(BF)
        g_z_copy[h] = send(g_out.at[:, wings[h]], g_z.at[:, wings[h]], "z")

    def top_stage(h):
        at = cut[h]
        g_z_copy[h].wait_recv()
        total = g_own[:, at] + g_z[:, at].astype(F32)
        top[top_quarter, at] = total
        t_out[:, at] = total.astype(BF)
        t_y_copy[h] = send(t_out.at[:, wings[h]], t_y.at[:, wings[h]], "y")
        place = top.at[top_quarter, wings[h]]
        t_core_copy[h] = send(place, place, "core")

    def last_stage(h):
        at = cut[h]
        t_y_copy[h].wait_recv()
        t_last[h] = send(t_y.at[:, wings[h]], t_core.at[:, wings[h]], "core")
        top[quarter_of(bits[0], 1 - bits[2]), at] = t_y[:, at].astype(F32)

    e_core_copy.wait_recv()
    g_half[...] = e_out[near_half, :].astype(F32) + e_core[...].astype(F32)
    y_stage(0)
    y_stage(1)
    z_stage(0)
    z_stage(1)
    stream.append(stream_chunk(wing // 2, wing + wing // 2))

    near_part(2, feat_in[1, :, :rows])

    top_stage(0)
    top_stage(1)
    o_z_copy.wait_recv()
    total = o_q[...] + o_z[...].astype(F32)
    omega[top_quarter, :] = total
    o_t[...] = total.astype(BF)
    o_t_copy = send(o_t, o_ty, "y")
    place = omega.at[top_quarter, :]
    o_own_copy = send(place, place, "core")
    last_stage(0)
    last_stage(1)
    o_t_copy.wait_recv()
    o_last = send(o_ty, o_tc, "core")
    omega[quarter_of(bits[0], 1 - bits[2]), :] = o_ty[...].astype(F32)
    for part in stream:
        for copy in part:
            copy.wait_recv()
    for at in cut:
        sample[:, at] = mdot(near[...], wide[:, at]).astype(BF)

    other = quarter_of(1 - bits[0], 1 - bits[2])
    for h in range(2):
        t_core_copy[h].wait_recv()
        t_last[h].wait_recv()
    top[other, :] = t_core[...].astype(F32)
    o_own_copy.wait_recv()
    o_last.wait_recv()
    omega[other, :] = o_tc[...].astype(F32)
    for copy in pending:
        copy.wait_send()


def write_out(a, b, c, a_out, b_out, c_out, sem):
    copies = [pltpu.make_async_copy(src, dst, sem.at[i])
              for i, (src, dst) in enumerate(((a, a_out), (b, b_out), (c, c_out)))]
    for copy in copies:
        copy.start()
    for copy in copies:
        copy.wait()


def on_device(n_blk, points, test_matrix, near_lists, leaf_pivots, leaf_proj, merge_pivots, merge_proj):
    rows, cols = test_matrix.shape
    rank = leaf_pivots.shape[1]
    slots = near_lists.shape[1]
    near_amp = 9.0 / math.sqrt(slots * (rows // near_lists.shape[0]))
    far_amp = 3.0 / math.sqrt(rank)
    half = rank // 2
    quarter = rank // 4
    vmem = pl.BlockSpec(memory_space=pltpu.VMEM)
    hbm = pl.BlockSpec(memory_space=pltpu.HBM)
    anyw = pl.BlockSpec(memory_space=pl.ANY)
    copies = 40
    scratch = [
        pltpu.VMEM(near_lists.shape, jnp.int32),
        pltpu.VMEM(points.shape, BF),
        pltpu.VMEM(leaf_pivots.shape, jnp.int32),
        pltpu.VMEM(merge_pivots.shape, jnp.int32),
        pltpu.VMEM(leaf_proj.shape, BF),
        pltpu.VMEM(merge_proj.shape, BF),
        pltpu.VMEM((3 * rows, cols), BF),
        pltpu.VMEM((3 * rank, cols), BF),
        pltpu.VMEM((rows, 3 * rows), BF),
        pltpu.VMEM((rank, 3 * rank), BF),
        pltpu.VMEM((16, rows + rank), BF),
        pltpu.VMEM((2, 16, rows + rank), BF),
        pltpu.VMEM((16, 3 * rank), BF),
        pltpu.VMEM((16, 3 * rank), BF),
        pltpu.VMEM((16, 2 * rank), BF),
        pltpu.VMEM((16, 2 * rank), BF),
        pltpu.VMEM((16, rank), BF),
        pltpu.VMEM((16, rank), BF),
        pltpu.VMEM((rank, cols), F32),
        pltpu.VMEM((half, cols), F32),
        pltpu.VMEM((half, cols), F32),
        pltpu.VMEM((quarter, cols), F32),
    ] + [pltpu.VMEM((quarter, cols), BF)] * 7 + [
        pltpu.VMEM((2, rank, cols), BF),
        pltpu.VMEM((2, half, cols), BF),
        pltpu.VMEM((2, half, cols), BF),
        pltpu.VMEM((2, half, cols), BF),
        pltpu.VMEM((rank, cols), BF),
        pltpu.VMEM((half, cols), BF),
        pltpu.VMEM((half, cols), F32),
        pltpu.VMEM((quarter, cols), F32),
    ] + [pltpu.VMEM((quarter, cols), BF)] * 7 + [
        pltpu.SemaphoreType.REGULAR((2,)),
        pltpu.SemaphoreType.DMA((7,)),
        pltpu.SemaphoreType.DMA((copies,)),
        pltpu.SemaphoreType.DMA((copies,)),
    ]
    shapes = (
        jax.ShapeDtypeStruct((rows, cols), BF),
        jax.ShapeDtypeStruct((rank, cols), F32),
        jax.ShapeDtypeStruct((rank, cols), F32),
    )
    operands = [
        pltpu.with_memory_space_constraint(v, pltpu.HBM)
        for v in (near_lists, points, leaf_pivots, merge_pivots, test_matrix, leaf_proj, merge_proj)
    ]
    made = pl.pallas_call(
        functools.partial(body, n_blk, near_amp, far_amp),
        name="hss",
        out_shape=shapes,
        in_specs=[hbm] * 7,
        out_specs=(vmem, vmem, vmem),
        scratch_shapes=scratch,
        compiler_params=pltpu.CompilerParams(
            collective_id=0, has_side_effects=True, vmem_limit_bytes=40 << 20),
    )(*operands)
    return pl.pallas_call(
        write_out,
        name="write_out",
        out_shape=shapes,
        in_specs=[anyw] * 3,
        out_specs=(anyw, anyw, anyw),
        scratch_shapes=[pltpu.SemaphoreType.DMA((3,))],
        compiler_params=pltpu.CompilerParams(vmem_limit_bytes=1 << 20),
    )(*made)


def solution(mesh):
    placed = (
        P(None, ("blk", "leaf")),
        P(("blk", "leaf"), None),
        P(("blk", "leaf"), None),
        P(("blk", "leaf"), None),
        P(("blk", "leaf"), None),
        P(None, ("blk", "leaf"), None),
        P(None, ("blk", "leaf"), None, None),
    )
    return jax.shard_map(
        functools.partial(on_device, mesh.shape["blk"]),
        mesh=mesh,
        in_specs=placed,
        out_specs=(P(("blk", "leaf"), None), P(("blk", "leaf"), None), P(("blk", "leaf"), None)),
        check_vma=False,
    )
```

```python
import functools
import math

import jax
import jax.numpy as jnp
from jax import lax
from jax.experimental import pallas as pl
from jax.experimental.pallas import tpu as pltpu
from jax.sharding import PartitionSpec as P

SPREAD = 25.0
MESH = pl.DeviceIdType.MESH
BF = jnp.bfloat16
F32 = jnp.float32
FAR = -512.0
SCALE = 2.0 * SPREAD / math.log(2.0)


def tdot(a, b):
    return lax.dot_general(a, b, (((0,), (0,)), ((), ())), preferred_element_type=F32)


def mdot(a, b):
    return jnp.dot(a, b, preferred_element_type=F32)


def rows_of(shape, entries):
    index = lax.broadcasted_iota(jnp.int32, shape, 0)
    result = jnp.zeros(shape, F32)
    for at, value in entries:
        result = jnp.where(index == at, value, result)
    return result


PLACES = ((9, 10), (14, 15), (12, 13))


def features(points, lists, block_rows):
    count = points.shape[1]
    x, y, z = points[0:1], points[1:2], points[2:3]
    half = 0.5 * (x * x + y * y + z * z)
    high = half.astype(BF).astype(F32)
    mid = (half - high).astype(BF).astype(F32)
    low = (half - high - mid).astype(BF).astype(F32)
    lane = lax.broadcasted_iota(jnp.int32, (1, count), 1)
    entries = [(0, x), (1, y), (2, z), (3, 1.0), (4, 1.0), (5, 1.0), (6, high), (7, mid), (8, low)]
    for place, at in enumerate(PLACES):
        for j in range(2):
            listed = jnp.max((lists == 2 * place + j).astype(F32), axis=1, keepdims=True)
            skipped = (1.0 - listed) * FAR
            entries.append((at[j], jnp.where(lane < block_rows, skipped[0:1], skipped[1:2])))
    return rows_of((16, count), entries)


def source_side(feat, place=None):
    r = lax.broadcasted_iota(jnp.int32, (16, 16), 0)
    c = lax.broadcasted_iota(jnp.int32, (16, 16), 1)
    same = (r == c) & (r < 3)
    swap = ((r >= 3) & (r < 6) & (c == r + 3)) | ((r >= 6) & (r < 9) & (c == r - 3))
    form = jnp.where(same, 1.0, jnp.where(swap, -1.0, 0.0)).astype(BF)
    turned = mdot(form, feat)
    count = feat.shape[1]
    extra = [(11, FAR)]
    if place is not None:
        lane = lax.broadcasted_iota(jnp.int32, (1, count), 1)
        first = (lane < count // 2).astype(F32)
        extra += [(PLACES[place][0], first), (PLACES[place][1], 1.0 - first)]
    return (turned + rows_of(turned.shape, extra)).astype(BF)


def only_valid(feat):
    index = lax.broadcasted_iota(jnp.int32, feat.shape, 0)
    return jnp.where(index == 11, 1.0 - feat[3:4], feat).astype(BF)


def kernel_of(target, source, amp):
    return jnp.exp2(tdot(target, source) * SCALE + math.log2(amp))


def one_hot(pivots, offset, count):
    k = lax.broadcasted_iota(jnp.int32, (count, pivots.shape[1]), 0)
    return jnp.where(k == pivots - offset, 1.0, 0.0).astype(BF)


def body(n_blk, near_amp, far_amp,
         lists_hbm, points_hbm, pivots_hbm, tree_pivots_hbm, test_hbm, proj_hbm, tree_hbm,
         sample, top, omega,
         lists, points, pivots, tree_pivots, proj, tree, wide, stack, near, far,
         feat_out, feat_in, kept_out, kept_in, chip_out, z_in, y_in, yz_in,
         o_out, o_core, o_sum, o_q, o_part, o_y, o_send, o_z, o_t, o_ty, o_tc,
         r_out, r_core, r_sum, r_x, e_out, e_core, g_half, g_own,
         g_part, g_y, g_out, g_z, t_out, t_y, t_core,
         hello, local_sem, send_sem, recv_sem):
    b = lax.axis_index("blk")
    l = lax.axis_index("leaf")
    bits = [lax.rem(l // (1 << t), 2) for t in range(3)]
    step = [(1 << t) - (2 << t) * bits[t] for t in range(3)]
    peers = {
        "next": {"blk": lax.rem(b + 1, n_blk), "leaf": l},
        "prev": {"blk": lax.rem(b + n_blk - 1, n_blk), "leaf": l},
        "core": {"blk": b, "leaf": l + step[0]},
        "z": {"blk": b, "leaf": l + step[1]},
        "y": {"blk": b, "leaf": l + step[2]},
        "yz": {"blk": b, "leaf": l + step[1] + step[2]},
    }
    barrier = pltpu.get_barrier_semaphore()
    upper = bits[1]
    for name in ("next", "prev", "core", "y"):
        pl.semaphore_signal(barrier, inc=1, device_id=peers[name], device_id_type=MESH)

    @pl.when(upper == 0)
    def _():
        for name in ("z", "yz"):
            pl.semaphore_signal(barrier, inc=1, device_id=peers[name], device_id_type=MESH)

    rows, rank = proj.shape
    block_rows = rows // 2
    half = rank // 2
    quarter = half // 2
    pending = []

    def plan(src, dst, peer):
        at = len(pending)
        copy = pltpu.make_async_remote_copy(
            src_ref=src, dst_ref=dst, send_sem=send_sem.at[at], recv_sem=recv_sem.at[at],
            device_id=peers[peer], device_id_type=MESH)
        pending.append(copy)
        return copy

    def send(src, dst, peer):
        copy = plan(src, dst, peer)
        copy.start()
        return copy

    def fetch(at, src, dst):
        copy = pltpu.make_async_copy(src, dst, local_sem.at[at])
        copy.start()
        return copy

    small = [fetch(0, lists_hbm, lists), fetch(1, points_hbm, points),
             fetch(2, pivots_hbm, pivots), fetch(3, tree_pivots_hbm, tree_pivots)]
    large = [fetch(4, test_hbm, wide.at[pl.ds(rows, rows), :]), fetch(5, proj_hbm, proj),
             fetch(6, tree_hbm, tree)]

    near_half = pl.ds(pl.multiple_of(bits[0] * half, half), half)
    far_half = pl.ds(pl.multiple_of((1 - bits[0]) * half, half), half)
    near_quarter = pl.ds(pl.multiple_of(bits[2] * quarter, quarter), quarter)
    far_quarter = pl.ds(pl.multiple_of((1 - bits[2]) * quarter, quarter), quarter)

    def quarter_of(core, part):
        return pl.ds(pl.multiple_of(core * half + part * quarter, quarter), quarter)

    top_quarter = quarter_of(bits[0], bits[2])

    for copy in small:
        copy.wait()
    own = features(points[...].astype(F32), lists[...], block_rows).astype(BF)
    skeleton = mdot(own, one_hot(pivots[...], 0, rows)).astype(BF)
    kept = skeleton
    for t in range(3):
        kept = mdot(kept, one_hot(tree_pivots[t], rank * bits[t], rank)).astype(BF)
        kept_out[:, t * rank:(t + 1) * rank] = kept
    feat_out[:, :rows] = own
    feat_out[:, rows:] = only_valid(kept.astype(F32))

    @pl.when(upper == 0)
    def _():
        pl.semaphore_wait(barrier, 4)

    @pl.when(upper == 1)
    def _():
        pl.semaphore_wait(barrier, 6)
        for at, name in enumerate(("z", "yz")):
            pl.semaphore_signal(hello.at[at], inc=1, device_id=peers[name], device_id_type=MESH)

    feat_copy = [send(feat_out, feat_in.at[0], "next"), send(feat_out, feat_in.at[1], "prev")]
    kept_copy = send(kept_out, kept_in, "core")

    cols = wide.shape[1]
    wing = cols // 2
    wings = [pl.ds(h * wing, wing) for h in range(2)]
    cut = [slice(h * wing, (h + 1) * wing) for h in range(2)]

    def stream_chunk(start, size):
        at = pl.ds(start, size)
        return [
            send(test_hbm.at[:, at], wide.at[pl.ds(0, rows), at], "next"),
            send(test_hbm.at[:, at], wide.at[pl.ds(2 * rows, rows), at], "prev"),
        ]

    stream = [stream_chunk(0, wing // 2)]

    kept_copy.wait_recv()
    chip = kept_out[...].astype(F32) + kept_in[...].astype(F32)
    level1 = chip[:, :rank].astype(BF)
    chip_out[...] = chip[:, rank:].astype(BF)
    last_rank = pl.ds(rank, rank)
    chip_copy = [
        plan(chip_out, z_in, "z"),
        plan(chip_out.at[:, last_rank], yz_in, "yz"),
        send(chip_out.at[:, last_rank], y_in, "y"),
    ]

    @pl.when(upper == 1)
    def _():
        for copy in chip_copy[:2]:
            copy.start()

    for copy in large:
        copy.wait()

    r_core_copy = []
    for side, place in ((0, 2), (1, 0)):
        feat_copy[side].wait_recv()
        weights = kernel_of(feat_in[side, :, rows:], source_side(own, place), near_amp).astype(BF)
        r_out[side] = mdot(weights, wide[rows:2 * rows, :]).astype(BF)
        r_core_copy.append(send(r_out.at[side, far_half, :], r_core.at[side], "core"))

    share = tdot(proj[...], wide[rows:2 * rows, :])
    for t in range(3):
        high = share.astype(BF)
        low = (share - high.astype(F32)).astype(BF)
        stack[t * rank:(t + 1) * rank, :] = high
        child = tree[t, 0, pl.ds(pl.multiple_of(rank * bits[t], rank), rank), :]
        share = tdot(child, high) + tdot(child, low)
    o_out[...] = share

    r_x_copy = [[], []]
    for side, name in ((0, "prev"), (1, "next")):
        r_core_copy[side].wait_recv()
        r_sum[side] = (r_out[side, near_half, :].astype(F32) + r_core[side].astype(F32)).astype(BF)
        for h, at in enumerate(wings):
            r_x_copy[h].append(send(r_sum.at[side, :, at], r_x.at[1 - side, :, at], name))
    o_core_copy = send(o_out.at[far_half, :], o_core, "core")

    def weigh(t, feat, source):
        at = slice(t * rank, (t + 1) * rank)
        far[:, at] = kernel_of(only_valid(feat), source_side(source), far_amp).astype(BF)

    def near_part(place, feat):
        at = slice(place * rows, (place + 1) * rows)
        near[:, at] = kernel_of(own, source_side(feat, place), near_amp).astype(BF)

    weigh(0, kept_in[:, 2 * rank:].astype(F32), skeleton)
    near_part(1, own)

    o_core_copy.wait_recv()
    o_sum[...] = o_out[near_half, :] + o_core[...]
    o_part[...] = o_sum[far_quarter, :].astype(BF)
    o_y_copy = send(o_part, o_y, "y")

    @pl.when(upper == 0)
    def _():
        for at in range(2):
            pl.semaphore_wait(hello.at[at], 1)
        for copy in chip_copy[:2]:
            copy.start()

    near_part(0, feat_in[0, :, :rows])

    for copy in chip_copy:
        copy.wait_recv()
    weigh(1, z_in[:, rank:].astype(F32), level1)
    level2 = (chip_out[:, :rank].astype(F32) + z_in[:, :rank].astype(F32)).astype(BF)
    weigh(2, y_in[...].astype(F32) + yz_in[...].astype(F32), level2)
    e_out[...] = mdot(far[...], stack[...]).astype(BF)
    e_core_copy = send(e_out.at[far_half, :], e_core, "core")
    o_y_copy.wait_recv()
    o_q[...] = o_sum[near_quarter, :] + o_y[...].astype(F32)
    o_send[...] = o_q[...].astype(BF)
    o_z_copy = send(o_send, o_z, "z")

    g_y_copy, g_z_copy, t_y_copy, t_core_copy, t_last = {}, {}, {}, {}, {}

    def y_stage(h):
        at = cut[h]
        for copy in r_x_copy[h]:
            copy.wait_recv()
        g_half[:, at] = r_x[0, :, at].astype(F32) + r_x[1, :, at].astype(F32) - g_half[:, at]
        g_part[:, at] = g_half[far_quarter, at].astype(BF)
        g_y_copy[h] = send(g_part.at[:, wings[h]], g_y.at[:, wings[h]], "y")

    def z_stage(h):
        at = cut[h]
        g_y_copy[h].wait_recv()
        g_own[:, at] = g_half[near_quarter, at] + g_y[:, at].astype(F32)
        g_out[:, at] = g_own[:, at].astype(BF)
        g_z_copy[h] = send(g_out.at[:, wings[h]], g_z.at[:, wings[h]], "z")

    def top_stage(h):
        at = cut[h]
        g_z_copy[h].wait_recv()
        total = g_own[:, at] + g_z[:, at].astype(F32)
        top[top_quarter, at] = total
        t_out[:, at] = total.astype(BF)
        t_y_copy[h] = send(t_out.at[:, wings[h]], t_y.at[:, wings[h]], "y")
        place = top.at[top_quarter, wings[h]]
        t_core_copy[h] = send(place, place, "core")

    def last_stage(h):
        at = cut[h]
        t_y_copy[h].wait_recv()
        t_last[h] = send(t_y.at[:, wings[h]], t_core.at[:, wings[h]], "core")
        top[quarter_of(bits[0], 1 - bits[2]), at] = t_y[:, at].astype(F32)

    e_core_copy.wait_recv()
    g_half[...] = e_out[near_half, :].astype(F32) + e_core[...].astype(F32)
    y_stage(0)
    y_stage(1)
    z_stage(0)
    z_stage(1)
    stream.append(stream_chunk(wing // 2, wing + wing // 2))

    near_part(2, feat_in[1, :, :rows])

    o_z_copy.wait_recv()
    total = o_q[...] + o_z[...].astype(F32)
    omega[top_quarter, :] = total
    o_t[...] = total.astype(BF)
    o_t_copy = send(o_t, o_ty, "y")
    place = omega.at[top_quarter, :]
    o_own_copy = send(place, place, "core")
    top_stage(0)
    top_stage(1)
    last_stage(0)
    last_stage(1)
    o_t_copy.wait_recv()
    o_last = send(o_ty, o_tc, "core")
    omega[quarter_of(bits[0], 1 - bits[2]), :] = o_ty[...].astype(F32)
    for part in stream:
        for copy in part:
            copy.wait_recv()
    for at in cut:
        sample[:, at] = mdot(near[...], wide[:, at]).astype(BF)

    other = quarter_of(1 - bits[0], 1 - bits[2])
    for h in range(2):
        t_core_copy[h].wait_recv()
        t_last[h].wait_recv()
    top[other, :] = t_core[...].astype(F32)
    o_own_copy.wait_recv()
    o_last.wait_recv()
    omega[other, :] = o_tc[...].astype(F32)
    for copy in pending:
        copy.wait_send()


def write_out(a, b, c, a_out, b_out, c_out, sem):
    copies = [pltpu.make_async_copy(src, dst, sem.at[i])
              for i, (src, dst) in enumerate(((a, a_out), (b, b_out), (c, c_out)))]
    for copy in copies:
        copy.start()
    for copy in copies:
        copy.wait()


def on_device(n_blk, points, test_matrix, near_lists, leaf_pivots, leaf_proj, merge_pivots, merge_proj):
    rows, cols = test_matrix.shape
    rank = leaf_pivots.shape[1]
    slots = near_lists.shape[1]
    near_amp = 9.0 / math.sqrt(slots * (rows // near_lists.shape[0]))
    far_amp = 3.0 / math.sqrt(rank)
    half = rank // 2
    quarter = rank // 4
    vmem = pl.BlockSpec(memory_space=pltpu.VMEM)
    hbm = pl.BlockSpec(memory_space=pltpu.HBM)
    anyw = pl.BlockSpec(memory_space=pl.ANY)
    copies = 40
    scratch = [
        pltpu.VMEM(near_lists.shape, jnp.int32),
        pltpu.VMEM(points.shape, BF),
        pltpu.VMEM(leaf_pivots.shape, jnp.int32),
        pltpu.VMEM(merge_pivots.shape, jnp.int32),
        pltpu.VMEM(leaf_proj.shape, BF),
        pltpu.VMEM(merge_proj.shape, BF),
        pltpu.VMEM((3 * rows, cols), BF),
        pltpu.VMEM((3 * rank, cols), BF),
        pltpu.VMEM((rows, 3 * rows), BF),
        pltpu.VMEM((rank, 3 * rank), BF),
        pltpu.VMEM((16, rows + rank), BF),
        pltpu.VMEM((2, 16, rows + rank), BF),
        pltpu.VMEM((16, 3 * rank), BF),
        pltpu.VMEM((16, 3 * rank), BF),
        pltpu.VMEM((16, 2 * rank), BF),
        pltpu.VMEM((16, 2 * rank), BF),
        pltpu.VMEM((16, rank), BF),
        pltpu.VMEM((16, rank), BF),
        pltpu.VMEM((rank, cols), F32),
        pltpu.VMEM((half, cols), F32),
        pltpu.VMEM((half, cols), F32),
        pltpu.VMEM((quarter, cols), F32),
    ] + [pltpu.VMEM((quarter, cols), BF)] * 7 + [
        pltpu.VMEM((2, rank, cols), BF),
        pltpu.VMEM((2, half, cols), BF),
        pltpu.VMEM((2, half, cols), BF),
        pltpu.VMEM((2, half, cols), BF),
        pltpu.VMEM((rank, cols), BF),
        pltpu.VMEM((half, cols), BF),
        pltpu.VMEM((half, cols), F32),
        pltpu.VMEM((quarter, cols), F32),
    ] + [pltpu.VMEM((quarter, cols), BF)] * 7 + [
        pltpu.SemaphoreType.REGULAR((2,)),
        pltpu.SemaphoreType.DMA((7,)),
        pltpu.SemaphoreType.DMA((copies,)),
        pltpu.SemaphoreType.DMA((copies,)),
    ]
    shapes = (
        jax.ShapeDtypeStruct((rows, cols), BF),
        jax.ShapeDtypeStruct((rank, cols), F32),
        jax.ShapeDtypeStruct((rank, cols), F32),
    )
    operands = [
        pltpu.with_memory_space_constraint(v, pltpu.HBM)
        for v in (near_lists, points, leaf_pivots, merge_pivots, test_matrix, leaf_proj, merge_proj)
    ]
    made = pl.pallas_call(
        functools.partial(body, n_blk, near_amp, far_amp),
        name="hss",
        out_shape=shapes,
        in_specs=[hbm] * 7,
        out_specs=(vmem, vmem, vmem),
        scratch_shapes=scratch,
        compiler_params=pltpu.CompilerParams(
            collective_id=0, has_side_effects=True, vmem_limit_bytes=40 << 20),
    )(*operands)
    return pl.pallas_call(
        write_out,
        name="write_out",
        out_shape=shapes,
        in_specs=[anyw] * 3,
        out_specs=(anyw, anyw, anyw),
        scratch_shapes=[pltpu.SemaphoreType.DMA((3,))],
        compiler_params=pltpu.CompilerParams(vmem_limit_bytes=1 << 20),
    )(*made)


def solution(mesh):
    placed = (
        P(None, ("blk", "leaf")),
        P(("blk", "leaf"), None),
        P(("blk", "leaf"), None),
        P(("blk", "leaf"), None),
        P(("blk", "leaf"), None),
        P(None, ("blk", "leaf"), None),
        P(None, ("blk", "leaf"), None, None),
    )
    return jax.shard_map(
        functools.partial(on_device, mesh.shape["blk"]),
        mesh=mesh,
        in_specs=placed,
        out_specs=(P(("blk", "leaf"), None), P(("blk", "leaf"), None), P(("blk", "leaf"), None)),
        check_vma=False,
    )
```
